128 devices in a mesh: section: 8 (over y, core), edge: 16 (over z, x).
Axes of the slice: x: 4, y: 4, z: 4, core: 2. Of those that a mesh axis runs over, the one named last changes fastest.
Arguments:
- layer_nodes: bfloat16 [8, 2, 256, 512], P('section'), may hold values from -6 to 6
- layer_edges: bfloat16 [8, 2, 4096, 512], P('section', None, 'edge'), may hold values from -6 to 6
- top_nodes: bfloat16 [2, 256, 512], replicated, may hold values from -1.5 to 1.5
- top_edges: bfloat16 [2, 4096, 512], P(None, 'edge'), may hold values from -1.5 to 1.5
- tile_blocks: int32 [2, 32, 2], P(None, 'edge'), may hold values from 0 to 1
- senders: int32 [2, 4096], P(None, 'edge'), may hold values from 0 to 127
- receivers: int32 [2, 4096], P(None, 'edge'), may hold values from 0 to 127
- w_send: bfloat16 [8, 512, 512], P('section'), may hold values from -0.0625 to 0.0625
- w_recv: bfloat16 [8, 512, 512], P('section'), may hold values from -0.0625 to 0.0625
- w_edge: bfloat16 [8, 512, 512], P('section'), may hold values from -0.25 to 0.25
- w_msg: bfloat16 [8, 512, 512], P('section'), may hold values from -0.125 to 0.125
- w_node: bfloat16 [8, 512, 512], P('section'), may hold values from -0.25 to 0.25
- w_agg: bfloat16 [8, 512, 512], P('section'), may hold values from -0.25 to 0.25
- w_out: bfloat16 [8, 512, 512], P('section'), may hold values from -0.125 to 0.125
Outputs:
- node_grads: bfloat16 [8, 2, 256, 512], P('section', None, 'edge')
- edge_grads: bfloat16 [8, 2, 4096, 512], P('section', None, 'edge')
- g_send: float32 [8, 512, 512], P('section', 'edge')
- g_recv: float32 [8, 512, 512], P('section', 'edge')
- g_edge: float32 [8, 512, 512], P('section', 'edge')
- g_msg: float32 [8, 512, 512], P('section', 'edge')
- g_node: float32 [8, 512, 512], P('section', 'edge')
- g_agg: float32 [8, 512, 512], P('section', 'edge')
- g_out: float32 [8, 512, 512], P('section', 'edge')
The draws below stay inside these ranges and needn't reach their ends.
All inputs are finite; a program needn't handle non-finite values.
Results may differ from the reference program's by a relative error of at most 0.029.
Values may be sent and summed in bfloat16 or wider, within the bound.
A program may use at most 64 MiB of HBM per device.

```python
import jax
import jax.numpy as jnp

D = 512
HIDDEN_SIZE = 512
BLOCK = 128
TILE_E = 128
MB = 2
NODE_BLOCKS = 2
LAYERS = 8
NODES_MB = 256
TILES = 32
EDGES = 4096


def with_ends(result, stream_key, low, top_value):
    extent = result.shape
    index_at = [jax.random.randint(jax.random.fold_in(stream_key, axis), (), 0, extent[axis]) for axis in range(len(extent))]
    result = result.at[tuple(index_at)].set(low)
    longest = extent.index(max(extent))
    index_at[longest] = (index_at[longest] + 1) % extent[longest]
    return result.at[tuple(index_at)].set(top_value)


def level_of(stream_key, shape, cuts, least, largest):
    level = 1.0
    for axis_at, shards_of in cuts:
        heights = jax.random.uniform(jax.random.fold_in(jax.random.fold_in(stream_key, 6), axis_at), (shards_of,), jnp.float32, least / len(cuts), largest / len(cuts))
        level = level * jnp.repeat(jnp.exp(heights), shape[axis_at] // shards_of).reshape((-1,) + (1,) * (len(shape) - 1 - axis_at))
    return level


def noise(rng, shape, scale, limit, cuts=(), held_as=jnp.bfloat16):
    gain = level_of(rng, shape, cuts, -0.22, 0.18) if cuts else 1.0
    drawn = jax.random.normal(rng, shape, jnp.float32) * scale * gain
    return jnp.minimum(jnp.maximum(drawn, -limit), limit).astype(held_as)


def setup_inputs(seed: int = 0) -> dict:
    key_of = jax.random.split(jax.random.key(seed), 15)
    layer_nodes = noise(key_of[0], (LAYERS, MB, NODES_MB, D), 1.0, 6.0, ((0, 8),))
    layer_edges = noise(key_of[1], (LAYERS, MB, EDGES, D), 1.0, 6.0, ((0, 8), (2, 16)))
    top_nodes = noise(key_of[2], (MB, NODES_MB, D), 0.25, 1.5)
    top_edges = noise(key_of[3], (MB, EDGES, D), 0.25, 1.5, ((1, 16),))
    tile_blocks = with_ends(jax.random.randint(key_of[4], (MB, TILES, 2), 0, NODE_BLOCKS), jax.random.fold_in(key_of[4], 1), 0, NODE_BLOCKS - 1).astype(jnp.int32)
    senders = with_ends(jax.random.randint(key_of[5], (MB, EDGES), 0, BLOCK), jax.random.fold_in(key_of[5], 1), 0, BLOCK - 1).astype(jnp.int32)
    receivers = with_ends(jax.random.randint(key_of[6], (MB, EDGES), 0, BLOCK), jax.random.fold_in(key_of[6], 1), 0, BLOCK - 1).astype(jnp.int32)
    w_send = noise(key_of[7], (LAYERS, D, HIDDEN_SIZE), (16 * D) ** -0.5, 0.0625, ((0, 8),))
    w_recv = noise(key_of[8], (LAYERS, D, HIDDEN_SIZE), (16 * D) ** -0.5, 0.0625, ((0, 8),))
    w_edge = noise(key_of[9], (LAYERS, D, HIDDEN_SIZE), D ** -0.5, 0.25, ((0, 8),))
    w_msg = noise(key_of[10], (LAYERS, HIDDEN_SIZE, D), (4 * HIDDEN_SIZE) ** -0.5, 0.125, ((0, 8),))
    w_node = noise(key_of[11], (LAYERS, D, HIDDEN_SIZE), D ** -0.5, 0.25, ((0, 8),))
    w_agg = noise(key_of[12], (LAYERS, D, HIDDEN_SIZE), D ** -0.5, 0.25, ((0, 8),))
    w_out = noise(key_of[13], (LAYERS, HIDDEN_SIZE, D), (4 * HIDDEN_SIZE) ** -0.5, 0.125, ((0, 8),))
    return dict(layer_nodes=layer_nodes, layer_edges=layer_edges, top_nodes=top_nodes, top_edges=top_edges, tile_blocks=tile_blocks, senders=senders, receivers=receivers, w_send=w_send, w_recv=w_recv, w_edge=w_edge, w_msg=w_msg, w_node=w_node, w_agg=w_agg, w_out=w_out)


def silu_slope(values):
    sigma = jax.nn.sigmoid(values)
    return sigma * (1.0 + values * (1.0 - sigma))


def matmul(left, right):
    return jnp.dot(left, right, preferred_element_type=jnp.float32)


def layer_back(feats, edge_feats, grad_nodes, grad_edges, send_index, recv_index, weights):
    w_send, w_recv, w_edge, w_msg, w_node, w_agg, w_out = weights
    send_feats = feats[send_index]
    recv_feats = feats[recv_index]
    pre = matmul(send_feats, w_send) + matmul(recv_feats, w_recv) + matmul(edge_feats, w_edge)
    act = jax.nn.silu(pre).astype(jnp.bfloat16)
    message = matmul(act, w_msg).astype(jnp.bfloat16)
    aggregate = jax.ops.segment_sum(message.astype(jnp.float32), recv_index, num_segments=NODES_MB)
    agg_b = aggregate.astype(jnp.bfloat16)
    node_pre = matmul(feats, w_node) + matmul(agg_b, w_agg)
    node_act = jax.nn.silu(node_pre).astype(jnp.bfloat16)
    node_delta = (matmul(grad_nodes, w_out.T) * silu_slope(node_pre)).astype(jnp.bfloat16)
    agg_grad = matmul(node_delta, w_agg.T).astype(jnp.bfloat16)
    message_grad = (grad_edges.astype(jnp.float32) + agg_grad[recv_index].astype(jnp.float32)).astype(jnp.bfloat16)
    edge_delta = (matmul(message_grad, w_msg.T) * silu_slope(pre)).astype(jnp.bfloat16)
    edge_out = (grad_edges.astype(jnp.float32) + matmul(edge_delta, w_edge.T)).astype(jnp.bfloat16)
    send_grad = matmul(edge_delta, w_send.T).astype(jnp.bfloat16)
    recv_grad = matmul(edge_delta, w_recv.T).astype(jnp.bfloat16)
    scattered = jax.ops.segment_sum(send_grad.astype(jnp.float32), send_index, num_segments=NODES_MB)
    scattered = scattered + jax.ops.segment_sum(recv_grad.astype(jnp.float32), recv_index, num_segments=NODES_MB)
    node_out = (grad_nodes.astype(jnp.float32) + matmul(node_delta, w_node.T) + scattered).astype(jnp.bfloat16)
    grads = (matmul(send_feats.T, edge_delta), matmul(recv_feats.T, edge_delta), matmul(edge_feats.T, edge_delta),
             matmul(act.T, message_grad), matmul(feats.T, node_delta), matmul(agg_b.T, node_delta),
             matmul(node_act.T, grad_nodes))
    return node_out, edge_out, grads


def reference(layer_nodes, layer_edges, top_nodes, top_edges, tile_blocks, senders, receivers,
              w_send, w_recv, w_edge, w_msg, w_node, w_agg, w_out):
    tile_of_edge = jnp.arange(EDGES, dtype=jnp.int32) // TILE_E
    node_table = [[None] * MB for layer in range(LAYERS)]
    edge_table = [[None] * MB for layer in range(LAYERS)]
    grad_table = [None] * LAYERS
    for batch in range(MB):
        send_index = (tile_blocks[batch, :, 0][tile_of_edge] * BLOCK + senders[batch]).astype(jnp.int32)
        recv_index = (tile_blocks[batch, :, 1][tile_of_edge] * BLOCK + receivers[batch]).astype(jnp.int32)
        grad_nodes = top_nodes[batch]
        grad_edges = top_edges[batch]
        for layer in reversed(range(LAYERS)):
            weights = (w_send[layer], w_recv[layer], w_edge[layer], w_msg[layer],
                       w_node[layer], w_agg[layer], w_out[layer])
            grad_nodes, grad_edges, grads = layer_back(layer_nodes[layer, batch], layer_edges[layer, batch],
                                                       grad_nodes, grad_edges, send_index, recv_index, weights)
            node_table[layer][batch] = grad_nodes
            edge_table[layer][batch] = grad_edges
            if grad_table[layer] is None:
                grad_table[layer] = grads
            else:
                grad_table[layer] = tuple(before + extra for before, extra in zip(grad_table[layer], grads))
    node_grads = jnp.stack([jnp.stack(node_table[layer]) for layer in range(LAYERS)])
    edge_grads = jnp.stack([jnp.stack(edge_table[layer]) for layer in range(LAYERS)])
    stacked = [jnp.stack([grad_table[layer][index] for layer in range(LAYERS)]) for index in range(7)]
    return (node_grads, edge_grads, stacked[0], stacked[1], stacked[2], stacked[3], stacked[4], stacked[5], stacked[6])
```

```python
import functools

import jax
import jax.numpy as jnp
from jax import lax
from jax.experimental import pallas as pl
from jax.experimental.pallas import tpu as pltpu
from jax.sharding import PartitionSpec as P

MESH = pl.DeviceIdType.MESH
BF = jnp.bfloat16
F32 = jnp.float32


def dot(left, right):
    return jnp.dot(left, right, preferred_element_type=F32)


def dot_t(left, right):
    return lax.dot_general(left, right, (((1,), (1,)), ((), ())), preferred_element_type=F32)


def take_bytes(ref, sem):
    pltpu.make_async_copy(ref, ref, sem).wait()


def kernel(
    sections,
    groups,
    nodes,
    edges,
    top_n,
    top_e,
    blocks,
    senders,
    receivers,
    w_send,
    w_recv,
    w_edge,
    w_msg,
    w_node,
    w_agg,
    w_out,
    node_out,
    edge_out,
    o_send,
    o_recv,
    o_edge,
    o_msg,
    o_node,
    o_agg,
    o_out,
    send_t,
    recv_t,
    recv_1,
    act,
    slope_e,
    slope_n,
    node_delta,
    base,
    w_am,
    nodes_t,
    edges_t,
    act_t,
    agg_t,
    node_act_t,
    total,
    agg_src,
    agg_buf,
    agg_row,
    agg_all,
    back_src,
    back_buf,
    row_src,
    gh,
    ge,
    grad_src,
    grad_buf,
    s_agg,
    r_agg,
    s_all,
    r_all,
    s_back,
    r_back,
    s_gh,
    r_gh,
    s_ge,
    r_ge,
    s_grad,
    r_grad,
):
    section = lax.axis_index("section")
    me = lax.axis_index("edge")
    batches, count, width = nodes.shape
    local = edges.shape[1]
    rows = count // groups
    share = width // groups
    first = section == sections - 1
    last = section == 0

    barrier = pltpu.get_barrier_semaphore()

    def greet(k, carry):
        pl.semaphore_signal(
            barrier, inc=1, device_id=(section, lax.rem(me + k, groups)), device_id_type=MESH
        )
        return carry

    lax.fori_loop(1, groups, greet, 0)

    @pl.when(section < sections - 1)
    def _():
        def greet_up(k, carry):
            pl.semaphore_signal(barrier, inc=1, device_id=(section + 1, k), device_id_type=MESH)
            return carry

        lax.fori_loop(0, groups, greet_up, 0)

    def scatter(src, dst, ssem, rsem):
        def one(k, carry):
            peer = lax.rem(me + k, groups)
            pltpu.make_async_remote_copy(
                src_ref=src.at[peer],
                dst_ref=dst.at[me],
                send_sem=ssem,
                recv_sem=rsem,
                device_id=(section, peer),
                device_id_type=MESH,
            ).start()
            return carry

        lax.fori_loop(1, groups, one, 0)

    def spread(src, dst, ssem, rsem, where, start):
        def one(k, carry):
            peer = lax.rem(me + k, groups)
            pltpu.make_async_remote_copy(
                src_ref=src,
                dst_ref=dst.at[me],
                send_sem=ssem,
                recv_sem=rsem,
                device_id=(where, peer),
                device_id_type=MESH,
            ).start()
            return carry

        lax.fori_loop(start, groups, one, 0)

    lane = lax.broadcasted_iota(jnp.int32, (1, local), 1)
    tile_len = local // blocks.shape[1]
    row_id = lax.broadcasted_iota(jnp.int32, (count, local), 0)
    for m in range(batches):
        for side, index, hot in ((0, senders, send_t), (1, receivers, recv_t)):
            block = jnp.zeros((1, local), jnp.int32)
            for k in range(blocks.shape[1]):
                block = jnp.where(lane // tile_len == k, blocks[m, k, side], block)
            ids = index[m : m + 1, :] + block * 128
            picked = jnp.where(row_id == ids, 1.0, 0.0).astype(F32)
            hot[m] = picked.astype(BF)
            if side == 1:
                recv_1[m] = picked.T.astype(BF)

    def forward(m, carry):
        feats = nodes[m]
        send_feats = lax.dot_general(
            send_t[m], feats, (((0,), (0,)), ((), ())), preferred_element_type=F32
        ).astype(BF)
        recv_feats = dot(recv_1[m], feats).astype(BF)
        pre = dot(send_feats, w_send[...]) + dot(recv_feats, w_recv[...]) + dot(edges[m], w_edge[...])
        sigma = jax.nn.sigmoid(pre)
        done = (pre * sigma).astype(BF)
        act[m] = done
        slope_e[m] = sigma * (1.0 + pre * (1.0 - sigma))
        message = dot(done, w_msg[...]).astype(BF)
        part = dot(recv_t[m], message)
        agg_src[m] = part.astype(BF).reshape(groups, rows, width)

        @pl.when(m == 0)
        def _():
            pl.semaphore_wait(barrier, groups - 1 + groups * (section > 0).astype(jnp.int32))

        scatter(agg_src.at[m], agg_buf.at[m], s_agg.at[m], r_agg.at[m])
        agg_buf[m, me] = agg_src[m, me]
        return carry

    lax.fori_loop(0, batches, forward, 0)

    w_am[...] = lax.dot_general(
        w_agg[...], w_msg[...], (((0,), (1,)), ((), ())), preferred_element_type=F32
    ).astype(BF)

    def gather_aggregate(m, carry):
        take_bytes(agg_buf.at[m, pl.ds(0, groups - 1)], r_agg.at[m])
        summed = jnp.sum(agg_buf[m].astype(F32), axis=0).astype(BF)
        agg_row[m] = summed
        agg_all[m, me] = summed
        spread(agg_row.at[m], agg_all.at[m], s_all.at[m], r_all.at[m], section, 1)
        return carry

    lax.fori_loop(0, batches, gather_aggregate, 0)

    def transposes():
        def one(m, carry):
            nodes_t[m] = nodes[m].T
            edges_t[m] = edges[m].T
            act_t[m] = act[m].T
            return carry

        lax.fori_loop(0, batches, one, 0)

    transposes()
    total[...] = jnp.zeros_like(total)
    for out in (o_node, o_agg, o_out):
        out[...] = jnp.zeros_like(out)

    def backward(m, carry):
        take_bytes(agg_all.at[m, pl.ds(0, groups - 1)], r_all.at[m])
        feats = nodes[m]
        agg_b = agg_all[m].reshape(count, width)
        node_pre = dot(feats, w_node[...]) + dot(agg_b, w_agg[...])
        sigma = jax.nn.sigmoid(node_pre)
        agg_t[...] = agg_b.T
        node_act_t[...] = (node_pre * sigma).astype(BF).T
        slope_n[...] = sigma * (1.0 + node_pre * (1.0 - sigma))

        @pl.when(first)
        def _():
            ge[m] = top_e[m]
            gh[m] = top_n[m].reshape(groups, rows, width)

        @pl.when(section < sections - 1)
        def _():
            take_bytes(ge.at[m], r_ge.at[m])

        base[...] = dot_t(ge[m], w_msg[...])

        @pl.when(section < sections - 1)
        def _():
            take_bytes(gh.at[m], r_gh.at[m])

        grad_nodes = gh[m].reshape(count, width)
        delta = (dot_t(grad_nodes, w_out[...]) * slope_n[...]).astype(BF)
        node_delta[...] = delta
        mixed = dot(delta, w_am[...]).astype(BF)
        edge_delta = ((base[...] + dot(recv_1[m], mixed)) * slope_e[m]).astype(BF)
        at_send = dot(send_t[m], edge_delta).astype(BF)
        at_recv = dot(recv_t[m], edge_delta).astype(BF)
        part = dot_t(at_send, w_send[...]) + dot_t(at_recv, w_recv[...])
        back_src[m] = part.astype(BF).reshape(groups, rows, width)
        scatter(back_src.at[m], back_buf.at[m], s_back.at[m], r_back.at[m])
        back_buf[m, me] = back_src[m, me]

        edge_out[m] = (ge[m].astype(F32) + dot_t(edge_delta, w_edge[...])).astype(BF)

        @pl.when(section > 0)
        def _():
            pltpu.make_async_remote_copy(
                src_ref=edge_out.at[m],
                dst_ref=ge.at[m],
                send_sem=s_ge.at[m],
                recv_sem=r_ge.at[m],
                device_id=(section - 1, me),
                device_id_type=MESH,
            ).start()

        own = node_delta[pl.ds(pl.multiple_of(me * rows, rows), rows), :]
        own_term = gh[m, me].astype(F32) + dot_t(own, w_node[...])

        take_bytes(back_buf.at[m, pl.ds(0, groups - 1)], r_back.at[m])
        summed = (own_term + jnp.sum(back_buf[m].astype(F32), axis=0)).astype(BF)
        node_out[m] = summed
        row_src[m] = summed

        @pl.when(section > 0)
        def _():
            spread(row_src.at[m], gh.at[m], s_gh.at[m], r_gh.at[m], section - 1, 0)

        agg_grad = dot_t(delta, w_agg[...]).astype(BF)
        message_grad = (ge[m].astype(F32) + dot(recv_1[m], agg_grad)).astype(BF)
        total[3] += dot(act_t[m], message_grad)
        total[2] += dot(edges_t[m], edge_delta)
        total[0] += dot(nodes_t[m], at_send)
        total[1] += dot(nodes_t[m], at_recv)
        piece = pl.ds(pl.multiple_of(me * share, share), share)
        o_node[...] += dot(nodes_t[m, piece, :], delta)
        o_agg[...] += dot(agg_t[piece, :], delta)
        o_out[...] += dot(node_act_t[piece, :], grad_nodes)
        return carry

    lax.fori_loop(0, batches, backward, 0)

    outs = (o_send, o_recv, o_edge, o_msg)
    order = (3, 2, 0, 1)
    for i in order:
        grad_src[i] = total[i].astype(BF).reshape(groups, share, width)
        scatter(grad_src.at[i], grad_buf.at[i], s_grad.at[i], r_grad.at[i])
        grad_buf[i, me] = grad_src[i, me]
    for i in order:
        take_bytes(grad_buf.at[i, pl.ds(0, groups - 1)], r_grad.at[i])
        outs[i][...] = jnp.sum(grad_buf[i].astype(F32), axis=0)

    for m in range(batches):
        take_bytes(agg_src.at[m, pl.ds(0, groups - 1)], s_agg.at[m])
        take_bytes(agg_all.at[m, pl.ds(0, groups - 1)], s_all.at[m])
        take_bytes(back_src.at[m, pl.ds(0, groups - 1)], s_back.at[m])

        @pl.when(section > 0)
        def _():
            take_bytes(edge_out.at[m], s_ge.at[m])
            take_bytes(gh.at[m], s_gh.at[m])

    for i in order:
        take_bytes(grad_src.at[i, pl.ds(0, groups - 1)], s_grad.at[i])


def body(sections, groups, *args):
    nodes, edges, top_n, top_e, blocks, senders, receivers, *weights = args
    weights = [w[0] for w in weights]
    nodes, edges = nodes[0], edges[0]
    batches, count, width = nodes.shape
    local = edges.shape[1]
    hidden = weights[0].shape[1]
    rows, share = count // groups, width // groups
    vmem = pl.BlockSpec(memory_space=pltpu.VMEM)
    smem = pl.BlockSpec(memory_space=pltpu.SMEM)
    full = (batches, groups, rows, width)
    sem = pltpu.SemaphoreType.DMA
    scratch = [
        pltpu.VMEM((batches, count, local), BF),
        pltpu.VMEM((batches, count, local), BF),
        pltpu.VMEM((batches, local, count), BF),
        pltpu.VMEM((batches, local, hidden), BF),
        pltpu.VMEM((batches, local, hidden), F32),
        pltpu.VMEM((count, hidden), F32),
        pltpu.VMEM((count, hidden), BF),
        pltpu.VMEM((local, hidden), F32),
        pltpu.VMEM((hidden, hidden), BF),
        pltpu.VMEM((batches, width, count), BF),
        pltpu.VMEM((batches, width, local), BF),
        pltpu.VMEM((batches, hidden, local), BF),
        pltpu.VMEM((width, count), BF),
        pltpu.VMEM((hidden, count), BF),
        pltpu.VMEM((4, width, hidden), F32),
        pltpu.VMEM(full, BF),
        pltpu.VMEM(full, BF),
        pltpu.VMEM((batches, rows, width), BF),
        pltpu.VMEM(full, BF),
        pltpu.VMEM(full, BF),
        pltpu.VMEM(full, BF),
        pltpu.VMEM((batches, rows, width), BF),
        pltpu.VMEM(full, BF),
        pltpu.VMEM((batches, local, width), BF),
        pltpu.VMEM((4, groups, share, hidden), BF),
        pltpu.VMEM((4, groups, share, hidden), BF),
    ] + [sem((batches,))] * 10 + [sem((4,))] * 2
    shapes = [
        jax.ShapeDtypeStruct((batches, rows, width), BF),
        jax.ShapeDtypeStruct((batches, local, width), BF),
    ] + [jax.ShapeDtypeStruct((share, hidden), F32)] * 7
    results = pl.pallas_call(
        functools.partial(kernel, sections, groups),
        out_shape=shapes,
        in_specs=[vmem] * 4 + [smem] + [vmem] * 9,
        out_specs=[vmem] * 9,
        scratch_shapes=scratch,
        compiler_params=pltpu.CompilerParams(
            collective_id=0, has_side_effects=True, vmem_limit_bytes=56 * 1024 * 1024
        ),
        name="window",
    )(nodes, edges, top_n, top_e, blocks, senders, receivers, *weights)
    return tuple(r[None] for r in results)


def solution(mesh):
    in_specs = (
        P("section", None, None, None),
        P("section", None, "edge", None),
        P(),
        P(None, "edge", None),
        P(None, "edge", None),
        P(None, "edge"),
        P(None, "edge"),
    ) + (P("section", None, None),) * 7
    out_specs = (
        P("section", None, "edge", None),
        P("section", None, "edge", None),
    ) + (P("section", "edge", None),) * 7
    step = functools.partial(body, mesh.shape["section"], mesh.shape["edge"])
    return jax.shard_map(step, mesh=mesh, in_specs=in_specs, out_specs=out_specs, check_vma=False)
```

```python
import functools

import jax
import jax.numpy as jnp
from jax import lax
from jax.experimental import pallas as pl
from jax.experimental.pallas import tpu as pltpu
from jax.sharding import PartitionSpec as P

MESH = pl.DeviceIdType.MESH
BF = jnp.bfloat16
F32 = jnp.float32


def dot(left, right):
    return jnp.dot(left, right, preferred_element_type=F32)


def dot_t(left, right):
    return lax.dot_general(left, right, (((1,), (1,)), ((), ())), preferred_element_type=F32)


def take_bytes(ref, sem):
    pltpu.make_async_copy(ref, ref, sem).wait()


def torus_offsets(side):
    def far(offset):
        return -sum(min(step, side - step) for step in offset)

    return sorted(((a, b) for a in range(side) for b in range(side)), key=far)


def kernel(sections, groups, batches, *refs):
    (
        h_nodes,
        h_edges,
        h_top_n,
        h_top_e,
        blocks,
        senders,
        receivers,
        h_send,
        h_recv,
        h_edge,
        h_msg,
        h_node,
        h_agg,
        h_out,
        h_node_out,
        h_edge_out,
        h_grads,
        nodes,
        edges,
        gh,
        ge,
        w_send,
        w_recv,
        w_edge,
        w_msg,
        w_node,
        w_agg,
        w_out,
        node_out,
        edge_out,
        grads,
        send_t,
        recv_t,
        recv_1,
        act,
        slope_e,
        slope_n,
        node_act,
        node_delta,
        edge_delta,
        at_send,
        at_recv,
        base,
        own_term,
        row_in,
        w_am,
        nodes_t,
        edges_t,
        act_t,
        sum_t,
        agg_t,
        node_act_t,
        agg_b,
        sum_src,
        sum_buf,
        sum_row,
        sum_all,
        back_src,
        back_buf,
        grad_src,
        grad_buf,
        s_load,
        s_store,
        s_sum,
        r_sum,
        s_all,
        r_all,
        s_back,
        r_back,
        s_gh,
        r_gh,
        s_row,
        r_row,
        s_ge,
        r_ge,
        s_grad,
        r_grad,
    ) = refs
    section = lax.axis_index("section")
    me = lax.axis_index("edge")
    count, width = nodes.shape[1:]
    local = edges.shape[1]
    rows = count // groups
    share = width // groups
    side = round(groups**0.5)
    first = section == sections - 1
    hops_down = jnp.logical_and(lax.rem(section, 2) == 0, section > 0)
    relays = jnp.logical_and(lax.rem(section, 2) == 1, section < sections - 1)
    offsets = torus_offsets(side)
    row_at, col_at = me // side, lax.rem(me, side)

    def peer_at(offset):
        return lax.rem(row_at + offset[0], side) * side + lax.rem(col_at + offset[1], side)

    barrier = pltpu.get_barrier_semaphore()
    for offset in offsets[:-1]:
        pl.semaphore_signal(
            barrier, inc=1, device_id=(section, peer_at(offset)), device_id_type=MESH
        )

    @pl.when(section < sections - 1)
    def _():
        for offset in offsets:
            pl.semaphore_signal(
                barrier, inc=1, device_id=(section + 1, peer_at(offset)), device_id_type=MESH
            )

    loads = [
        pltpu.make_async_copy(src, dst, s_load.at[i])
        for i, (src, dst) in enumerate(
            (
                (h_nodes, nodes),
                (h_edges, edges),
                (h_send, w_send),
                (h_recv, w_recv),
                (h_edge, w_edge),
                (h_msg, w_msg),
                (h_node, w_node),
                (h_agg, w_agg),
                (h_out, w_out),
            )
        )
    ]
    for copy in loads:
        copy.start()
    tops = [
        pltpu.make_async_copy(h_top_n, gh, s_load.at[len(loads)]),
        pltpu.make_async_copy(h_top_e, ge, s_load.at[len(loads) + 1]),
    ]

    @pl.when(first)
    def _():
        for copy in tops:
            copy.start()

    def scatter(src, dst, ssem, rsem):
        for offset in offsets[:-1]:
            peer = peer_at(offset)
            pltpu.make_async_remote_copy(
                src_ref=src.at[peer],
                dst_ref=dst.at[me],
                send_sem=ssem,
                recv_sem=rsem,
                device_id=(section, peer),
                device_id_type=MESH,
            ).start()

    def spread(src, dst, ssem, rsem, where, targets):
        for offset in targets:
            pltpu.make_async_remote_copy(
                src_ref=src,
                dst_ref=dst,
                send_sem=ssem,
                recv_sem=rsem,
                device_id=(where, peer_at(offset)),
                device_id_type=MESH,
            ).start()

    lane = lax.broadcasted_iota(jnp.int32, (1, local), 1)
    tile_len = local // blocks.shape[1]
    row_id = lax.broadcasted_iota(jnp.int32, (count, local), 0)
    for m in range(batches):
        for part, index, hot in ((0, senders, send_t), (1, receivers, recv_t)):
            block = jnp.zeros((1, local), jnp.int32)
            for k in range(blocks.shape[1]):
                block = jnp.where(lane // tile_len == k, blocks[m, k, part], block)
            ids = index[m : m + 1, :] + block * 128
            picked = jnp.where(row_id == ids, 1.0, 0.0).astype(F32)
            hot[m] = picked.astype(BF)
            if part == 1:
                recv_1[m] = picked.T.astype(BF)

    for copy in loads[:5]:
        copy.wait()
    mine = pl.ds(pl.multiple_of(me * rows, rows), rows)
    piece = pl.ds(pl.multiple_of(me * share, share), share)

    for m in range(batches):
        feats = nodes[m]
        send_feats = lax.dot_general(
            send_t[m], feats, (((0,), (0,)), ((), ())), preferred_element_type=F32
        ).astype(BF)
        recv_feats = dot(recv_1[m], feats).astype(BF)
        pre = dot(send_feats, w_send[...]) + dot(recv_feats, w_recv[...]) + dot(edges[m], w_edge[...])
        sigma = jax.nn.sigmoid(pre)
        done = (pre * sigma).astype(BF)
        act[m] = done
        slope_e[m] = sigma * (1.0 + pre * (1.0 - sigma))
        sum_src[m] = dot(recv_t[m], done).astype(BF).reshape(groups, rows, width)
        if m == 0:
            pl.semaphore_wait(barrier, groups - 1 + groups * (section > 0).astype(jnp.int32))
        scatter(sum_src.at[m], sum_buf.at[m], s_sum.at[m], r_sum.at[m])
        sum_buf[m, me] = sum_src[m, me]

    for copy in loads[5:]:
        copy.wait()
    w_am[...] = lax.dot_general(
        w_agg[...], w_msg[...], (((0,), (1,)), ((), ())), preferred_element_type=F32
    ).astype(BF)

    for m in range(batches):
        take_bytes(sum_buf.at[m, pl.ds(0, groups - 1)], r_sum.at[m])
        summed = jnp.sum(sum_buf[m].astype(F32), axis=0).astype(BF)
        sum_row[m] = summed
        spread(sum_row.at[m], sum_all.at[m, me], s_all.at[m], r_all.at[m], section, offsets[:-1])
        sum_all[m, me] = summed

    def node_forward(m):
        take_bytes(sum_all.at[m, pl.ds(0, groups - 1)], r_all.at[m])
        agg = dot(sum_all[m].reshape(count, width), w_msg[...]).astype(BF)
        agg_b[m] = agg
        node_pre = dot(nodes[m], w_node[...]) + dot(agg, w_agg[...])
        sigma = jax.nn.sigmoid(node_pre)
        node_act[m] = (node_pre * sigma).astype(BF)
        slope_n[m] = sigma * (1.0 + node_pre * (1.0 - sigma))

    def transposes():
        for m in range(batches):
            at = pl.ds(m * local, local)
            nodes_t[:, m * count : (m + 1) * count] = nodes[m].T
            edges_t[:, at] = edges[m].T
            act_t[:, at] = act[m].T
            sum_t[:, m * count : (m + 1) * count] = sum_all[m].reshape(count, width).T
            agg_t[:, m * count : (m + 1) * count] = agg_b[m].T
            node_act_t[:, m * count : (m + 1) * count] = node_act[m].T

    def edge_base(m):
        base[m] = dot_t(ge[m], w_msg[...])

    def chain(m):
        span = pl.ds(m * local, local)
        at = pl.ds(m * count, count)
        grad_nodes = gh[m].reshape(count, width)
        delta = (dot_t(grad_nodes, w_out[...]) * slope_n[m]).astype(BF)
        node_delta[at, :] = delta
        mixed = dot(delta, w_am[...]).astype(BF)
        moved = ((base[m] + dot(recv_1[m], mixed)) * slope_e[m]).astype(BF)
        edge_delta[span, :] = moved
        to_send = dot(send_t[m], moved).astype(BF)
        to_recv = dot(recv_t[m], moved).astype(BF)
        at_send[at, :] = to_send
        at_recv[at, :] = to_recv
        part = dot_t(to_send, w_send[...]) + dot_t(to_recv, w_recv[...])
        back_src[m] = part.astype(BF).reshape(groups, rows, width)
        scatter(back_src.at[m], back_buf.at[m], s_back.at[m], r_back.at[m])
        back_buf[m, me] = back_src[m, me]

        edge_out[m] = (ge[m].astype(F32) + dot_t(edge_delta[span, :], w_edge[...])).astype(BF)

        @pl.when(section > 0)
        def _():
            pltpu.make_async_remote_copy(
                src_ref=edge_out.at[m],
                dst_ref=ge.at[m],
                send_sem=s_ge.at[m],
                recv_sem=r_ge.at[m],
                device_id=(section - 1, me),
                device_id_type=MESH,
            ).start()

    def own_terms(m):
        own = node_delta[pl.ds(pl.multiple_of(m * count + me * rows, rows), rows), :]
        own_term[m] = gh[m, me].astype(F32) + dot_t(own, w_node[...])

    def finish(m):
        take_bytes(back_buf.at[m, pl.ds(0, groups - 1)], r_back.at[m])
        node_out[m] = (own_term[m] + jnp.sum(back_buf[m].astype(F32), axis=0)).astype(BF)

        @pl.when(lax.rem(section, 2) == 1)
        def _():
            spread(node_out.at[m], gh.at[m, me], s_gh.at[m], r_gh.at[m], section - 1, offsets)

        @pl.when(hops_down)
        def _():
            pltpu.make_async_remote_copy(
                src_ref=node_out.at[m],
                dst_ref=row_in.at[m],
                send_sem=s_row.at[m],
                recv_sem=r_row.at[m],
                device_id=(section - 1, me),
                device_id_type=MESH,
            ).start()

    def relay(m):
        @pl.when(relays)
        def _():
            take_bytes(row_in.at[m], r_row.at[m])
            spread(row_in.at[m], gh.at[m, me], s_gh.at[m], r_gh.at[m], section, offsets[:-1])
            gh[m, me] = row_in[m]

    def take_nodes(m):
        @pl.when(relays)
        def _():
            take_bytes(gh.at[m, pl.ds(0, groups - 1)], r_gh.at[m])

        @pl.when(lax.rem(section, 2) == 0)
        def _():
            take_bytes(gh.at[m], r_gh.at[m])

    def make_grad(i, value):
        grad_src[i] = value.astype(BF).reshape(groups, share, width)

    def send_grad(i):
        scatter(grad_src.at[i], grad_buf.at[i], s_grad.at[i], r_grad.at[i])

    node_forward(0)

    @pl.when(first)
    def _():
        for copy in tops:
            copy.wait()

    @pl.when(section < sections - 1)
    def _():
        node_forward(1)
        transposes()
        take_bytes(ge.at[0], r_ge.at[0])

    edge_base(0)

    @pl.when(section < sections - 1)
    def _():
        relay(0)
        take_bytes(ge.at[1], r_ge.at[1])
        edge_base(1)
        relay(1)
        make_grad(3, dot(act_t[...], ge[...].reshape(batches * local, width)))
        take_nodes(0)

    chain(0)

    @pl.when(first)
    def _():
        node_forward(1)
        edge_base(1)

    @pl.when(section < sections - 1)
    def _():
        take_nodes(1)

    @pl.when(section == 0)
    def _():
        send_grad(3)

    chain(1)

    @pl.when(first)
    def _():
        transposes()
        make_grad(3, dot(act_t[...], ge[...].reshape(batches * local, width)))

    make_grad(2, dot(edges_t[...], edge_delta[...]))

    @pl.when(section == 0)
    def _():
        send_grad(2)

    make_grad(0, dot(nodes_t[...], at_send[...]))

    @pl.when(section == 0)
    def _():
        send_grad(0)

    own_terms(0)
    own_terms(1)

    @pl.when(section > 0)
    def _():
        finish(0)

    make_grad(1, dot(nodes_t[...], at_recv[...]))

    @pl.when(section == 0)
    def _():
        send_grad(1)
        finish(0)

    finish(1)

    @pl.when(section > 0)
    def _():
        for i in (3, 2, 0, 1):
            send_grad(i)

    store_node = pltpu.make_async_copy(node_out, h_node_out, s_store.at[0])
    store_edge = pltpu.make_async_copy(edge_out, h_edge_out, s_store.at[1])
    store_node.start()
    store_edge.start()

    agg_grad = dot_t(node_delta[...], w_agg[...]).astype(BF)
    grads[4] = dot(nodes_t[piece, :], node_delta[...])
    grads[5] = dot(agg_t[piece, :], node_delta[...])
    grads[6] = dot(node_act_t[piece, :], gh[...].reshape(batches * count, width))
    known = dot(sum_t[piece, :], agg_grad)
    for i in (3, 2, 0, 1):
        grad_buf[i, me] = grad_src[i, me]
    for i in (3, 2, 0, 1):
        take_bytes(grad_buf.at[i, pl.ds(0, groups - 1)], r_grad.at[i])
        total = jnp.sum(grad_buf[i].astype(F32), axis=0)
        grads[i] = total + known if i == 3 else total
    store_grads = pltpu.make_async_copy(grads, h_grads, s_store.at[2])
    store_grads.start()

    for m in range(batches):
        take_bytes(sum_src.at[m, pl.ds(0, groups - 1)], s_sum.at[m])
        take_bytes(sum_all.at[m, pl.ds(0, groups - 1)], s_all.at[m])
        take_bytes(back_src.at[m, pl.ds(0, groups - 1)], s_back.at[m])

        @pl.when(section > 0)
        def _():
            take_bytes(edge_out.at[m], s_ge.at[m])

        @pl.when(lax.rem(section, 2) == 1)
        def _():
            take_bytes(gh.at[m], s_gh.at[m])

        @pl.when(hops_down)
        def _():
            take_bytes(row_in.at[m], s_row.at[m])

        @pl.when(relays)
        def _():
            take_bytes(gh.at[m, pl.ds(0, groups - 1)], s_gh.at[m])

    for i in range(4):
        take_bytes(grad_src.at[i, pl.ds(0, groups - 1)], s_grad.at[i])
    store_node.wait()
    store_edge.wait()
    store_grads.wait()


def write_kernel(*refs):
    node_in, edge_in, grads, node_out, edge_out, *outs, sems = refs
    copies = [
        pltpu.make_async_copy(edge_in, edge_out, sems.at[0]),
        pltpu.make_async_copy(node_in, node_out, sems.at[1]),
    ]
    copies += [
        pltpu.make_async_copy(grads.at[i], out, sems.at[2 + i]) for i, out in enumerate(outs)
    ]
    for copy in copies:
        copy.start()
    for copy in copies:
        copy.wait()


def body(sections, groups, *args):
    nodes, edges, top_n, top_e, blocks, senders, receivers, *weights = args
    weights = [w[0] for w in weights]
    nodes, edges = nodes[0], edges[0]
    batches, count, width = nodes.shape
    local = edges.shape[1]
    hidden = weights[0].shape[1]
    rows, share = count // groups, width // groups
    vmem = pl.BlockSpec(memory_space=pltpu.VMEM)
    smem = pl.BlockSpec(memory_space=pltpu.SMEM)
    anyw = pl.BlockSpec(memory_space=pl.ANY)
    full = (batches, groups, rows, width)
    sem = pltpu.SemaphoreType.DMA
    V = pltpu.VMEM
    node_shape = jax.ShapeDtypeStruct((batches, rows, width), BF)
    edge_shape = jax.ShapeDtypeStruct((batches, local, width), BF)
    grad_shape = jax.ShapeDtypeStruct((share, hidden), F32)
    scratch = (
        [V((batches, count, width), BF), V((batches, local, width), BF)]
        + [V(full, BF), V((batches, local, width), BF)]
        + [V(w.shape, BF) for w in weights]
        + [V((batches, rows, width), BF), V((batches, local, width), BF)]
        + [V((7, share, hidden), F32)]
        + [V((batches, count, local), BF), V((batches, count, local), BF)]
        + [V((batches, local, count), BF), V((batches, local, hidden), BF)]
        + [V((batches, local, hidden), F32), V((batches, count, hidden), F32)]
        + [V((batches, count, hidden), BF)]
        + [V((batches * count, hidden), BF), V((batches * local, hidden), BF)]
        + [V((batches * count, hidden), BF), V((batches * count, hidden), BF)]
        + [V((batches, local, hidden), F32), V((batches, rows, width), F32)]
        + [V((batches, rows, width), BF), V((hidden, hidden), BF)]
        + [V((width, batches * count), BF), V((width, batches * local), BF)]
        + [V((hidden, batches * local), BF), V((hidden, batches * count), BF)]
        + [V((width, batches * count), BF), V((hidden, batches * count), BF)]
        + [V((batches, count, width), BF)]
        + [V(full, BF), V(full, BF), V((batches, rows, width), BF), V(full, BF)]
        + [V(full, BF), V(full, BF)]
        + [V((4, groups, share, hidden), BF), V((4, groups, share, hidden), BF)]
        + [sem((11,)), sem((3,))]
        + [sem((batches,))] * 12
        + [sem((4,))] * 2
    )
    node_res, edge_res, grads = pl.pallas_call(
        functools.partial(kernel, sections, groups, batches),
        out_shape=[node_shape, edge_shape, jax.ShapeDtypeStruct((7, share, hidden), F32)],
        in_specs=[anyw] * 4 + [smem] + [vmem] * 2 + [anyw] * 7,
        out_specs=[anyw] * 3,
        scratch_shapes=scratch,
        compiler_params=pltpu.CompilerParams(
            collective_id=0, has_side_effects=True, vmem_limit_bytes=58 * 1024 * 1024
        ),
        name="window",
    )(
        nodes,
        edges,
        top_n.reshape(full),
        top_e,
        blocks,
        senders,
        receivers,
        *weights,
    )
    results = pl.pallas_call(
        write_kernel,
        out_shape=[node_shape, edge_shape] + [grad_shape] * 7,
        in_specs=[vmem] * 3,
        out_specs=[anyw] * 9,
        scratch_shapes=[sem((9,))],
        name="write",
    )(node_res, edge_res, grads)
    return tuple(r[None] for r in results)


def solution(mesh):
    in_specs = (
        P("section", None, None, None),
        P("section", None, "edge", None),
        P(),
        P(None, "edge", None),
        P(None, "edge", None),
        P(None, "edge"),
        P(None, "edge"),
    ) + (P("section", None, None),) * 7
    out_specs = (
        P("section", None, "edge", None),
        P("section", None, "edge", None),
    ) + (P("section", "edge", None),) * 7
    step = functools.partial(body, mesh.shape["section"], mesh.shape["edge"])
    return jax.shard_map(step, mesh=mesh, in_specs=in_specs, out_specs=out_specs, check_vma=False)
```

```python
import functools

import jax
import jax.numpy as jnp
from jax import lax
from jax.experimental import pallas as pl
from jax.experimental.pallas import tpu as pltpu
from jax.sharding import PartitionSpec as P

MESH = pl.DeviceIdType.MESH
BF = jnp.bfloat16
F32 = jnp.float32


def dot(left, right):
    return jnp.dot(left, right, preferred_element_type=F32)


def dot_t(left, right):
    return lax.dot_general(left, right, (((1,), (1,)), ((), ())), preferred_element_type=F32)


def take_bytes(ref, sem):
    pltpu.make_async_copy(ref, ref, sem).wait()


def torus_offsets(side):
    def far(offset):
        return -sum(min(step, side - step) for step in offset)

    return sorted(((a, b) for a in range(side) for b in range(side)), key=far)


def kernel(sections, groups, batches, *refs):
    (
        h_nodes,
        h_edges,
        h_top_n,
        h_top_e,
        blocks,
        senders,
        receivers,
        h_send,
        h_recv,
        h_edge,
        h_msg,
        h_node,
        h_agg,
        h_out,
        h_node_out,
        h_edge_out,
        h_grads,
        nodes,
        edges,
        gh,
        ge,
        w_send,
        w_recv,
        w_edge,
        w_msg,
        w_node,
        w_agg,
        w_out,
        w_am,
        node_out,
        edge_out,
        grads,
        send_t,
        recv_t,
        recv_1,
        act,
        slope_e,
        slope_n,
        node_act,
        node_delta,
        edge_delta,
        at_send,
        at_recv,
        base,
        own_term,
        row_in,
        nodes_t,
        edges_t,
        act_t,
        sum_t,
        agg_t,
        node_act_t,
        sum_src,
        sum_buf,
        sum_row,
        sum_all,
        back_src,
        back_buf,
        grad_src,
        grad_mid,
        half_src,
        half_buf,
        s_load,
        s_store,
        s_sum,
        r_sum,
        s_all,
        r_all,
        s_back,
        r_back,
        s_gh,
        r_gh,
        s_row,
        r_row,
        s_ge,
        r_ge,
        s_mate,
        r_mate,
        s_grad,
        r_grad,
        s_half,
        r_half,
        turn,
    ) = refs
    section = lax.axis_index("section")
    me = lax.axis_index("edge")
    count, width = nodes.shape[1:]
    local = edges.shape[1]
    rows = count // groups
    share = width // groups
    side = round(groups**0.5)
    odd = lax.rem(section, 2) == 1
    even = lax.rem(section, 2) == 0
    mate = section + 1 - 2 * lax.rem(section, 2)
    first = section == sections - 1
    later = jnp.logical_and(odd, section < sections - 1)
    hands_down = jnp.logical_and(odd, section > 1)
    offsets = torus_offsets(side)
    row_at, col_at = me // side, lax.rem(me, side)

    def peer_at(offset):
        return lax.rem(row_at + offset[0], side) * side + lax.rem(col_at + offset[1], side)

    def remote(src, dst, ssem, rsem, where, peer):
        return pltpu.make_async_remote_copy(
            src_ref=src,
            dst_ref=dst,
            send_sem=ssem,
            recv_sem=rsem,
            device_id=(where, peer),
            device_id_type=MESH,
        )

    barrier = pltpu.get_barrier_semaphore()
    for offset in offsets[:-1]:
        pl.semaphore_signal(
            barrier, inc=1, device_id=(section, peer_at(offset)), device_id_type=MESH
        )
    pl.semaphore_signal(barrier, inc=1, device_id=(mate, me), device_id_type=MESH)

    @pl.when(later)
    def _():
        pl.semaphore_signal(barrier, inc=1, device_id=(section + 2, me), device_id_type=MESH)

    loads = [
        pltpu.make_async_copy(src, dst, s_load.at[i])
        for i, (src, dst) in enumerate(
            (
                (h_nodes, nodes),
                (h_edges, edges),
                (h_send, w_send.at[0]),
                (h_recv, w_recv.at[0]),
                (h_edge, w_edge.at[0]),
                (h_msg, w_msg.at[0]),
                (h_node, w_node.at[0]),
                (h_agg, w_agg),
                (h_out, w_out.at[0]),
            )
        )
    ]
    for copy in loads:
        copy.start()
    tops = [
        pltpu.make_async_copy(h_top_n, gh.at[0], s_load.at[len(loads)]),
        pltpu.make_async_copy(h_top_e, ge, s_load.at[len(loads) + 1]),
    ]

    @pl.when(first)
    def _():
        for copy in tops:
            copy.start()

    def scatter(src, dst, ssem, rsem):
        for offset in offsets[:-1]:
            peer = peer_at(offset)
            remote(src.at[peer], dst.at[me], ssem, rsem, section, peer).start()

    def spread(src, dst, ssem, rsem):
        for offset in offsets[:-1]:
            remote(src, dst, ssem, rsem, section, peer_at(offset)).start()

    def hand(src, dst, i):
        remote(src, dst, s_mate.at[i], r_mate.at[i], mate, me).start()

    lane = lax.broadcasted_iota(jnp.int32, (1, local), 1)
    tile_len = local // blocks.shape[1]
    row_id = lax.broadcasted_iota(jnp.int32, (count, local), 0)
    piece = pl.ds(pl.multiple_of(me * share, share), share)

    for m in range(batches):
        for part, index, hot in ((0, senders, send_t), (1, receivers, recv_t)):
            block = jnp.zeros((1, local), jnp.int32)
            for k in range(blocks.shape[1]):
                block = jnp.where(lane // tile_len == k, blocks[m, k, part], block)
            ids = index[m : m + 1, :] + block * 128
            picked = jnp.where(row_id == ids, 1.0, 0.0).astype(F32)
            hot[m] = picked.astype(BF)
            if part == 1:
                recv_1[m] = picked.T.astype(BF)
        if m == 0:
            for copy in loads[:5]:
                copy.wait()
        feats = nodes[m]
        send_feats = lax.dot_general(
            send_t[m], feats, (((0,), (0,)), ((), ())), preferred_element_type=F32
        ).astype(BF)
        recv_feats = dot(recv_1[m], feats).astype(BF)
        pre = (
            dot(send_feats, w_send[0]) + dot(recv_feats, w_recv[0]) + dot(edges[m], w_edge[0])
        )
        sigma = jax.nn.sigmoid(pre)
        done = (pre * sigma).astype(BF)
        act[m] = done
        slope_e[0, m] = sigma * (1.0 + pre * (1.0 - sigma))
        sum_src[m] = dot(recv_t[m], done).astype(BF).reshape(groups, rows, width)
        if m == 0:
            pl.semaphore_wait(barrier, groups + hands_down.astype(jnp.int32))
        sum_buf[m, me] = sum_src[m, me]

        @pl.when(odd)
        def _():
            scatter(sum_src.at[m], sum_buf.at[m], s_sum.at[m], r_sum.at[m])

    for copy in loads[5:]:
        copy.wait()
    w_am[0] = lax.dot_general(
        w_agg[...], w_msg[0], (((0,), (1,)), ((), ())), preferred_element_type=F32
    ).astype(BF)
    down = (w_msg, w_send, w_recv, w_edge, w_node, w_out, w_am)

    @pl.when(even)
    def _():
        for i, w in enumerate(down):
            hand(w.at[0], w.at[1], i)
        for m in range(batches):
            hand(slope_e.at[0, m], slope_e.at[1, m], 7 + m)
        pl.semaphore_wait(turn, 1)
        for m in range(batches):
            scatter(sum_src.at[m], sum_buf.at[m], s_sum.at[m], r_sum.at[m])

    for m in range(batches):
        slope_n[0, m] = dot(nodes[m], w_node[0])

    @pl.when(first)
    def _():
        for copy in tops:
            copy.wait()
        for m in range(batches):
            base[m] = dot_t(ge[m], w_msg[0])

    for m in range(batches):
        take_bytes(sum_buf.at[m, pl.ds(0, groups - 1)], r_sum.at[m])
        summed = jnp.sum(sum_buf[m].astype(F32), axis=0).astype(BF)
        sum_row[m] = summed
        spread(sum_row.at[m], sum_all.at[m, me], s_all.at[m], r_all.at[m])
        sum_all[m, me] = summed

    @pl.when(odd)
    def _():
        pl.semaphore_signal(turn, inc=1, device_id=(mate, me), device_id_type=MESH)

    def node_forward(m):
        take_bytes(sum_all.at[m, pl.ds(0, groups - 1)], r_all.at[m])
        node_pre = slope_n[0, m] + dot_t(sum_all[m].reshape(count, width), w_am[0])
        sigma = jax.nn.sigmoid(node_pre)
        node_act[m] = (node_pre * sigma).astype(BF)
        slope_n[0, m] = sigma * (1.0 + node_pre * (1.0 - sigma))

        @pl.when(even)
        def _():
            hand(slope_n.at[0, m], slope_n.at[1, m], 9 + m)

    def transposes():
        for m in range(batches):
            at = pl.ds(m * local, local)
            nodes_t[:, m * count : (m + 1) * count] = nodes[m].T
            edges_t[:, at] = edges[m].T
            act_t[:, at] = act[m].T
            sum_t[:, m * count : (m + 1) * count] = sum_all[m].reshape(count, width).T
            agg = dot(sum_all[m].reshape(count, width), w_msg[0]).astype(BF)
            agg_t[:, m * count : (m + 1) * count] = agg.T
            node_act_t[:, m * count : (m + 1) * count] = node_act[m].T

    def edge_grad(li, m):
        return ge[m] if li == 0 else edge_out[0, m]

    def edge_base(li, m):
        base[m] = dot_t(edge_grad(li, m), w_msg[li])

    def chain(li, m):
        slot = li * batches + m
        span = pl.ds(m * local, local)
        at = pl.ds(m * count, count)
        grad_nodes = gh[li, m].reshape(count, width)
        delta = (dot_t(grad_nodes, w_out[li]) * slope_n[li, m]).astype(BF)
        node_delta[li, at, :] = delta
        mixed = dot(delta, w_am[li]).astype(BF)
        moved = ((base[m] + dot(recv_1[m], mixed)) * slope_e[li, m]).astype(BF)
        edge_delta[li, span, :] = moved
        if li == 1:

            @pl.when(section == 1)
            def _():
                hand(edge_delta.at[1, span], edge_delta.at[0, span], 2 + m)

        to_send = dot(send_t[m], moved).astype(BF)
        to_recv = dot(recv_t[m], moved).astype(BF)
        at_send[li, at, :] = to_send
        at_recv[li, at, :] = to_recv
        part = dot_t(to_send, w_send[li]) + dot_t(to_recv, w_recv[li])
        back_src[slot] = part.astype(BF).reshape(groups, rows, width)
        scatter(back_src.at[slot], back_buf.at[slot], s_back.at[slot], r_back.at[slot])
        back_buf[slot, me] = back_src[slot, me]
        if li == 1:

            @pl.when(section == 1)
            def _():
                hand_rest(m)

        edge_out[li, m] = (
            edge_grad(li, m).astype(F32) + dot_t(edge_delta[li, span, :], w_edge[li])
        ).astype(BF)
        if li == 0:
            hand(edge_out.at[0, m], ge.at[m], m)
        elif m == 0:

            @pl.when(section > 1)
            def _():
                edges_down(m)

    def hand_rest(m):
        at = pl.ds(m * count, count)
        hand(at_send.at[1, at], at_send.at[0, at], 4 + m)
        hand(at_recv.at[1, at], at_recv.at[0, at], 6 + m)
        hand(node_delta.at[1, at], node_delta.at[0, at], 8 + m)
        hand(gh.at[1, m], gh.at[0, m], 10 + m)

    def edges_down(m):
        remote(edge_out.at[1, m], ge.at[m], s_ge.at[m], r_ge.at[m], section - 2, me).start()

    def own_terms(li, m):
        own = node_delta[li, pl.ds(pl.multiple_of(m * count + me * rows, rows), rows), :]
        own_term[m] = gh[li, m, me].astype(F32) + dot_t(own, w_node[li])

    def finish(li, m):
        slot = li * batches + m
        take_bytes(back_buf.at[slot, pl.ds(0, groups - 1)], r_back.at[slot])
        summed = (own_term[m] + jnp.sum(back_buf[slot].astype(F32), axis=0)).astype(BF)
        node_out[li, m] = summed
        if li == 0:
            spread(node_out.at[0, m], gh.at[1, m, me], s_gh.at[2 + m], r_gh.at[2 + m])
            gh[1, m, me] = summed
        else:

            @pl.when(section > 1)
            def _():
                remote(
                    node_out.at[1, m], row_in.at[m], s_row.at[m], r_row.at[m], section - 2, me
                ).start()

            hand(node_out.at[1, m], node_out.at[0, m], 12 + m)

    def relay(m):
        take_bytes(row_in.at[m], r_row.at[m])
        spread(row_in.at[m], gh.at[0, m, me], s_gh.at[m], r_gh.at[m])
        gh[0, m, me] = row_in[m]

    def take_nodes(li, m):
        take_bytes(gh.at[li, m, pl.ds(0, groups - 1)], r_gh.at[li * batches + m])

    def make_grad(i):
        if i == 3:
            value = dot(act_t[...], ge[...].reshape(batches * local, width))
        elif i == 2:
            value = dot(edges_t[...], edge_delta[0])
        else:
            value = dot(nodes_t[...], (at_send if i == 0 else at_recv)[0])
        value = value.astype(BF)
        wide = width // 2
        left = value[:, :wide].reshape(side, side, share, wide)
        for k in range(side):
            grad_src[2 * i, k] = left[:, k]
        grad_src[2 * i + 1] = value[:, wide:].reshape(side, side, share, wide)

    steps = sorted(range(1, side), key=lambda step: -min(step, side - step))

    def along(half, step):
        return lax.rem((row_at if half else col_at) + step, side)

    def peer_along(half, spot):
        return spot * side + col_at if half else row_at * side + spot

    def send_grad(i):
        for half in range(2):
            slot = 2 * i + half
            for step in steps:
                spot = along(half, step)
                remote(
                    grad_src.at[slot, spot],
                    grad_mid.at[slot, along(half, 0)],
                    s_grad.at[slot],
                    r_grad.at[slot],
                    section,
                    peer_along(half, spot),
                ).start()

    def pass_grad(i):
        for half in range(2):
            slot = 2 * i + half
            here = along(half, 0)
            grad_mid[slot, here] = grad_src[slot, here]
            take_bytes(grad_mid.at[slot, pl.ds(0, side - 1)], r_grad.at[slot])
            half_src[slot] = jnp.sum(grad_mid[slot].astype(F32), axis=0).astype(BF)
            for step in steps:
                spot = along(1 - half, step)
                remote(
                    half_src.at[slot, spot],
                    half_buf.at[slot, along(1 - half, 0)],
                    s_half.at[slot],
                    r_half.at[slot],
                    section,
                    peer_along(1 - half, spot),
                ).start()
            half_buf[slot, along(1 - half, 0)] = half_src[slot, along(1 - half, 0)]

    node_forward(0)

    @pl.when(section < sections - 1)
    def _():
        node_forward(1)
        transposes()

    @pl.when(odd)
    def _():
        @pl.when(later)
        def _():
            take_bytes(ge.at[0], r_ge.at[0])
            edge_base(0, 0)
            relay(0)
            relay(1)
            take_nodes(0, 0)

        chain(0, 0)

        @pl.when(first)
        def _():
            node_forward(1)

        @pl.when(later)
        def _():
            take_bytes(ge.at[1], r_ge.at[1])
            edge_base(0, 1)
            take_nodes(0, 1)

        chain(0, 1)
        own_terms(0, 0)
        own_terms(0, 1)
        for i, w in enumerate(down):
            take_bytes(w.at[1], r_mate.at[i])
        edge_base(1, 0)
        edge_base(1, 1)
        finish(0, 0)
        finish(0, 1)

        @pl.when(first)
        def _():
            transposes()

        for i in (3, 2, 0, 1):
            make_grad(i)

            @pl.when(section == 1)
            def _():
                send_grad(i)

        for m in range(batches):
            take_bytes(slope_e.at[1, m], r_mate.at[7 + m])
            take_bytes(slope_n.at[1, m], r_mate.at[9 + m])
        take_nodes(1, 0)
        chain(1, 0)
        take_nodes(1, 1)
        chain(1, 1)
        own_terms(1, 0)
        own_terms(1, 1)
        finish(1, 0)

        @pl.when(section > 1)
        def _():
            edges_down(1)

        finish(1, 1)

        @pl.when(section > 1)
        def _():
            for m in range(batches):
                span = pl.ds(m * local, local)
                hand(edge_delta.at[1, span], edge_delta.at[0, span], 2 + m)
                hand_rest(m)

        for m in range(batches):
            hand(edge_out.at[1, m], edge_out.at[0, m], 14 + m)

        @pl.when(section > 1)
        def _():
            for i in (3, 2, 0, 1):
                send_grad(i)

    def take_outs():
        for m in range(batches):
            take_bytes(node_out.at[0, m], r_mate.at[12 + m])
            take_bytes(edge_out.at[0, m], r_mate.at[14 + m])

    @pl.when(even)
    def _():
        for m in range(batches):
            take_bytes(ge.at[m], r_mate.at[m])
        make_grad(3)
        last = section == 0
        for i, ref, at in ((2, edge_delta, 2), (0, at_send, 4), (1, at_recv, 6)):
            for m in range(batches):
                take_bytes(ref.at[0, pl.ds(m * local, local)], r_mate.at[at + m])
                if i == 2 and m == 0:

                    @pl.when(last)
                    def _():
                        send_grad(3)

            make_grad(i)

            @pl.when(last)
            def _():
                send_grad(i)

        for m in range(batches):
            take_bytes(node_delta.at[0, pl.ds(m * count, count)], r_mate.at[8 + m])
            take_bytes(gh.at[0, m], r_mate.at[10 + m])

        @pl.when(section > 0)
        def _():
            take_outs()
            for i in (3, 2, 0, 1):
                send_grad(i)

    agg_grad = dot_t(node_delta[0], w_agg[...]).astype(BF)
    grads[4] = dot(nodes_t[piece, :], node_delta[0])
    grads[5] = dot(agg_t[piece, :], node_delta[0])
    grads[6] = dot(node_act_t[piece, :], gh[0].reshape(batches * count, width))
    known = dot(sum_t[piece, :], agg_grad)
    for i in (3, 2, 0, 1):
        pass_grad(i)

    @pl.when(section == 0)
    def _():
        take_outs()

    store_node = pltpu.make_async_copy(node_out.at[0], h_node_out, s_store.at[0])
    store_edge = pltpu.make_async_copy(edge_out.at[0], h_edge_out, s_store.at[1])
    store_node.start()
    store_edge.start()
    for i in (3, 2, 0, 1):
        for half in range(2):
            slot = 2 * i + half
            lanes = slice(half * (width // 2), (half + 1) * (width // 2))
            take_bytes(half_buf.at[slot, pl.ds(0, side - 1)], r_half.at[slot])
            total = jnp.sum(half_buf[slot].astype(F32), axis=0)
            grads[i, :, lanes] = total + known[:, lanes] if i == 3 else total
    store_grads = pltpu.make_async_copy(grads, h_grads, s_store.at[2])
    store_grads.start()

    for m in range(batches):
        take_bytes(sum_src.at[m, pl.ds(0, groups - 1)], s_sum.at[m])
        take_bytes(sum_all.at[m, pl.ds(0, groups - 1)], s_all.at[m])

    @pl.when(even)
    def _():
        for i, w in enumerate(down):
            take_bytes(w.at[0], s_mate.at[i])
        for m in range(batches):
            take_bytes(slope_e.at[0, m], s_mate.at[7 + m])
            take_bytes(slope_n.at[0, m], s_mate.at[9 + m])

    @pl.when(odd)
    def _():
        for m in range(batches):
            for li in range(2):
                slot = li * batches + m
                take_bytes(back_src.at[slot, pl.ds(0, groups - 1)], s_back.at[slot])
            take_bytes(gh.at[1, m, pl.ds(0, groups - 1)], s_gh.at[2 + m])
            take_bytes(ge.at[m], s_mate.at[m])
            for ref, at in ((edge_delta, 2), (at_send, 4), (at_recv, 6), (node_delta, 8)):
                take_bytes(ref.at[1, pl.ds(m * local, local)], s_mate.at[at + m])
            take_bytes(gh.at[1, m], s_mate.at[10 + m])
            take_bytes(node_out.at[1, m], s_mate.at[12 + m])
            take_bytes(edge_out.at[1, m], s_mate.at[14 + m])

        @pl.when(section > 1)
        def _():
            for m in range(batches):
                take_bytes(row_in.at[m], s_row.at[m])
                take_bytes(ge.at[m], s_ge.at[m])

        @pl.when(later)
        def _():
            for m in range(batches):
                take_bytes(gh.at[0, m, pl.ds(0, groups - 1)], s_gh.at[m])

    for slot in range(8):
        take_bytes(grad_src.at[slot, pl.ds(0, side - 1)], s_grad.at[slot])
        take_bytes(half_src.at[slot, pl.ds(0, side - 1)], s_half.at[slot])
    store_node.wait()
    store_edge.wait()
    store_grads.wait()


def write_kernel(*refs):
    node_in, edge_in, grads, node_out, edge_out, *outs = refs[:-5]
    node_at, edge_at, grad_at, sem_in, sem_out = refs[-5:]
    moves = [(edge_in.at[m], edge_at.at[m], edge_out.at[m]) for m in range(edge_in.shape[0])]
    moves += [(node_in, node_at, node_out)]
    moves += [(grads.at[i], grad_at.at[i], out) for i, out in enumerate(outs)]
    ins = [pltpu.make_async_copy(a, b, sem_in.at[i]) for i, (a, b, _) in enumerate(moves)]
    outs = [pltpu.make_async_copy(b, c, sem_out.at[i]) for i, (_, b, c) in enumerate(moves)]
    for copy in ins:
        copy.start()
    for copy, after in zip(ins, outs):
        copy.wait()
        after.start()
    for copy in outs:
        copy.wait()


def body(sections, groups, *args):
    nodes, edges, top_n, top_e, blocks, senders, receivers, *weights = args
    weights = [w[0] for w in weights]
    nodes, edges = nodes[0], edges[0]
    batches, count, width = nodes.shape
    local = edges.shape[1]
    hidden = weights[0].shape[1]
    rows, share = count // groups, width // groups
    vmem = pl.BlockSpec(memory_space=pltpu.VMEM)
    smem = pl.BlockSpec(memory_space=pltpu.SMEM)
    anyw = pl.BlockSpec(memory_space=pl.ANY)
    full = (batches, groups, rows, width)
    sem = pltpu.SemaphoreType.DMA
    V = pltpu.VMEM
    node_shape = jax.ShapeDtypeStruct((batches, rows, width), BF)
    edge_shape = jax.ShapeDtypeStruct((batches, local, width), BF)
    grad_shape = jax.ShapeDtypeStruct((share, hidden), F32)
    pair = (2, batches)
    side = round(groups**0.5)
    scratch = (
        [V((batches, count, width), BF), V((batches, local, width), BF)]
        + [V((2,) + full, BF), V((batches, local, width), BF)]
        + [V(w.shape if i == 5 else (2,) + w.shape, BF) for i, w in enumerate(weights)]
        + [V((2, hidden, hidden), BF)]
        + [V(pair + (rows, width), BF), V(pair + (local, width), BF)]
        + [V((7, share, hidden), F32)]
        + [V((batches, count, local), BF), V((batches, count, local), BF)]
        + [V((batches, local, count), BF), V((batches, local, hidden), BF)]
        + [V(pair + (local, hidden), F32), V(pair + (count, hidden), F32)]
        + [V((batches, count, hidden), BF)]
        + [V((2, batches * count, hidden), BF), V((2, batches * local, hidden), BF)]
        + [V((2, batches * count, hidden), BF), V((2, batches * count, hidden), BF)]
        + [V((batches, local, hidden), F32), V((batches, rows, width), F32)]
        + [V((batches, rows, width), BF)]
        + [V((width, batches * count), BF), V((width, batches * local), BF)]
        + [V((hidden, batches * local), BF), V((hidden, batches * count), BF)]
        + [V((width, batches * count), BF), V((hidden, batches * count), BF)]
        + [V(full, BF), V(full, BF), V((batches, rows, width), BF), V(full, BF)]
        + [V((2 * batches,) + full[1:], BF), V((2 * batches,) + full[1:], BF)]
        + [V((8, side, side, share, hidden // 2), BF)] * 2
        + [V((8, side, share, hidden // 2), BF)] * 2
        + [sem((11,)), sem((3,))]
        + [sem((batches,))] * 4
        + [sem((2 * batches,))] * 4
        + [sem((batches,))] * 4
        + [sem((16,))] * 2
        + [sem((8,))] * 4
        + [pltpu.SemaphoreType.REGULAR]
    )
    node_res, edge_res, grads = pl.pallas_call(
        functools.partial(kernel, sections, groups, batches),
        out_shape=[node_shape, edge_shape, jax.ShapeDtypeStruct((7, share, hidden), F32)],
        in_specs=[anyw] * 4 + [smem] + [vmem] * 2 + [anyw] * 7,
        out_specs=[anyw] * 3,
        scratch_shapes=scratch,
        compiler_params=pltpu.CompilerParams(
            collective_id=0, has_side_effects=True, vmem_limit_bytes=58 * 1024 * 1024
        ),
        name="window",
    )(
        nodes,
        edges,
        top_n.reshape(full),
        top_e,
        blocks,
        senders,
        receivers,
        *weights,
    )
    results = pl.pallas_call(
        write_kernel,
        out_shape=[node_shape, edge_shape] + [grad_shape] * 7,
        in_specs=[anyw] * 3,
        out_specs=[anyw] * 9,
        scratch_shapes=[
            V(node_shape.shape, BF),
            V(edge_shape.shape, BF),
            V((7, share, hidden), F32),
            sem((batches + 8,)),
            sem((batches + 8,)),
        ],
        name="write",
    )(node_res, edge_res, grads)
    return tuple(r[None] for r in results)


def solution(mesh):
    in_specs = (
        P("section", None, None, None),
        P("section", None, "edge", None),
        P(),
        P(None, "edge", None),
        P(None, "edge", None),
        P(None, "edge"),
        P(None, "edge"),
    ) + (P("section", None, None),) * 7
    out_specs = (
        P("section", None, "edge", None),
        P("section", None, "edge", None),
    ) + (P("section", "edge", None),) * 7
    step = functools.partial(body, mesh.shape["section"], mesh.shape["edge"])
    return jax.shard_map(step, mesh=mesh, in_specs=in_specs, out_specs=out_specs, check_vma=False)
```

```python
import functools

import jax
import jax.numpy as jnp
from jax import lax
from jax.experimental import pallas as pl
from jax.experimental.pallas import tpu as pltpu
from jax.sharding import PartitionSpec as P

MESH = pl.DeviceIdType.MESH
BF = jnp.bfloat16
F32 = jnp.float32


def dot(left, right):
    return jnp.dot(left, right, preferred_element_type=F32)


def dot_t(left, right):
    return lax.dot_general(left, right, (((1,), (1,)), ((), ())), preferred_element_type=F32)


def take_bytes(ref, sem):
    pltpu.make_async_copy(ref, ref, sem).wait()


def torus_offsets(side):
    def far(offset):
        return -sum(min(step, side - step) for step in offset)

    return sorted(((a, b) for a in range(side) for b in range(side)), key=far)


def kernel(sections, groups, batches, *refs):
    (
        h_nodes,
        h_edges,
        h_top_n,
        h_top_e,
        blocks,
        senders,
        receivers,
        h_send,
        h_recv,
        h_edge,
        h_msg,
        h_node,
        h_agg,
        h_out,
        h_node_out,
        h_edge_out,
        h_grads,
        nodes,
        edges,
        gh,
        ge,
        w_send,
        w_recv,
        w_edge,
        w_msg,
        w_node,
        w_agg,
        w_out,
        w_am,
        node_out,
        edge_out,
        grads,
        send_t,
        recv_t,
        recv_1,
        act,
        slope_e,
        slope_n,
        node_act,
        node_delta,
        edge_delta,
        at_send,
        at_recv,
        base,
        own_term,
        row_in,
        nodes_t,
        edges_t,
        act_t,
        sum_t,
        agg_t,
        node_act_t,
        sum_src,
        sum_buf,
        sum_row,
        sum_all,
        back_src,
        back_buf,
        grad_src,
        grad_mid,
        half_src,
        half_buf,
        s_load,
        s_store,
        s_sum,
        r_sum,
        s_all,
        r_all,
        s_back,
        r_back,
        s_gh,
        r_gh,
        s_row,
        r_row,
        s_ge,
        r_ge,
        s_mate,
        r_mate,
        s_grad,
        r_grad,
        s_half,
        r_half,
        turn,
    ) = refs
    section = lax.axis_index("section")
    me = lax.axis_index("edge")
    count, width = nodes.shape[1:]
    local = edges.shape[1]
    rows = count // groups
    share = width // groups
    side = round(groups**0.5)
    odd = lax.rem(section, 2) == 1
    even = lax.rem(section, 2) == 0
    mate = section + 1 - 2 * lax.rem(section, 2)
    first = section == sections - 1
    later = jnp.logical_and(odd, section < sections - 1)
    hands_down = jnp.logical_and(odd, section > 1)
    offsets = torus_offsets(side)
    row_at, col_at = me // side, lax.rem(me, side)

    def peer_at(offset):
        return lax.rem(row_at + offset[0], side) * side + lax.rem(col_at + offset[1], side)

    def remote(src, dst, ssem, rsem, where, peer):
        return pltpu.make_async_remote_copy(
            src_ref=src,
            dst_ref=dst,
            send_sem=ssem,
            recv_sem=rsem,
            device_id=(where, peer),
            device_id_type=MESH,
        )

    barrier = pltpu.get_barrier_semaphore()
    for offset in offsets[:-1]:
        pl.semaphore_signal(
            barrier, inc=1, device_id=(section, peer_at(offset)), device_id_type=MESH
        )
    pl.semaphore_signal(barrier, inc=1, device_id=(mate, me), device_id_type=MESH)

    @pl.when(later)
    def _():
        pl.semaphore_signal(barrier, inc=1, device_id=(section + 2, me), device_id_type=MESH)

    loads = [
        pltpu.make_async_copy(src, dst, s_load.at[i])
        for i, (src, dst) in enumerate(
            (
                (h_nodes, nodes),
                (h_edges, edges),
                (h_send, w_send.at[0]),
                (h_recv, w_recv.at[0]),
                (h_edge, w_edge.at[0]),
                (h_msg, w_msg.at[0]),
                (h_node, w_node.at[0]),
                (h_agg, w_agg),
                (h_out, w_out.at[0]),
            )
        )
    ]
    for copy in loads[:5]:
        copy.start()
    tops = [
        pltpu.make_async_copy(h_top_n, gh.at[0], s_load.at[len(loads)]),
        pltpu.make_async_copy(h_top_e, ge, s_load.at[len(loads) + 1]),
    ]


    def scatter(src, dst, ssem, rsem):
        for offset in offsets[:-1]:
            peer = peer_at(offset)
            remote(src.at[peer], dst.at[me], ssem, rsem, section, peer).start()

    def spread(src, dst, ssem, rsem):
        for offset in offsets[:-1]:
            remote(src, dst, ssem, rsem, section, peer_at(offset)).start()

    def hand(src, dst, i):
        remote(src, dst, s_mate.at[i], r_mate.at[i], mate, me).start()

    lane = lax.broadcasted_iota(jnp.int32, (1, local), 1)
    tile_len = local // blocks.shape[1]
    row_id = lax.broadcasted_iota(jnp.int32, (count, local), 0)
    piece = pl.ds(pl.multiple_of(me * share, share), share)

    for m in range(batches):
        for part, index, hot in ((0, senders, send_t), (1, receivers, recv_t)):
            block = jnp.zeros((1, local), jnp.int32)
            for k in range(blocks.shape[1]):
                block = jnp.where(lane // tile_len == k, blocks[m, k, part], block)
            ids = index[m : m + 1, :] + block * 128
            picked = jnp.where(row_id == ids, 1.0, 0.0).astype(F32)
            hot[m] = picked.astype(BF)
            if part == 1:
                recv_1[m] = picked.T.astype(BF)
        if m == 0:
            for copy in loads[:5]:
                copy.wait()
            for copy in loads[5:]:
                copy.start()

            @pl.when(first)
            def _():
                for copy in tops:
                    copy.start()

        feats = nodes[m]
        send_feats = lax.dot_general(
            send_t[m], feats, (((0,), (0,)), ((), ())), preferred_element_type=F32
        ).astype(BF)
        recv_feats = dot(recv_1[m], feats).astype(BF)
        pre = (
            dot(send_feats, w_send[0]) + dot(recv_feats, w_recv[0]) + dot(edges[m], w_edge[0])
        )
        sigma = jax.nn.sigmoid(pre)
        done = (pre * sigma).astype(BF)
        act[m] = done
        slope_e[0, m] = sigma * (1.0 + pre * (1.0 - sigma))
        sum_src[m] = dot(recv_t[m], done).astype(BF).reshape(groups, rows, width)
        if m == 0:
            pl.semaphore_wait(barrier, groups + hands_down.astype(jnp.int32))
        sum_buf[m, me] = sum_src[m, me]

        @pl.when(odd)
        def _():
            scatter(sum_src.at[m], sum_buf.at[m], s_sum.at[m], r_sum.at[m])
            if m == batches - 1:
                pl.semaphore_signal(turn, inc=1, device_id=(mate, me), device_id_type=MESH)

    for copy in loads[5:]:
        copy.wait()
    w_am[0] = lax.dot_general(
        w_agg[...], w_msg[0], (((0,), (1,)), ((), ())), preferred_element_type=F32
    ).astype(BF)
    down = (w_msg, w_send, w_recv, w_edge, w_node, w_out, w_am)

    @pl.when(even)
    def _():
        for i, w in enumerate(down):
            hand(w.at[0], w.at[1], i)
        for m in range(batches):
            hand(slope_e.at[0, m], slope_e.at[1, m], 7 + m)
        pl.semaphore_wait(turn, 1)
        for m in range(batches):
            scatter(sum_src.at[m], sum_buf.at[m], s_sum.at[m], r_sum.at[m])

    for m in range(batches):
        slope_n[0, m] = dot(nodes[m], w_node[0])

    @pl.when(first)
    def _():
        for copy in tops:
            copy.wait()
        for m in range(batches):
            base[m] = dot_t(ge[m], w_msg[0])

    for m in range(batches):
        take_bytes(sum_buf.at[m, pl.ds(0, groups - 1)], r_sum.at[m])
        summed = jnp.sum(sum_buf[m].astype(F32), axis=0).astype(BF)
        sum_row[m] = summed
        spread(sum_row.at[m], sum_all.at[m, me], s_all.at[m], r_all.at[m])
        sum_all[m, me] = summed

    def node_forward(m):
        take_bytes(sum_all.at[m, pl.ds(0, groups - 1)], r_all.at[m])
        node_pre = slope_n[0, m] + dot_t(sum_all[m].reshape(count, width), w_am[0])
        sigma = jax.nn.sigmoid(node_pre)
        node_act[m] = (node_pre * sigma).astype(BF)
        slope_n[0, m] = sigma * (1.0 + node_pre * (1.0 - sigma))

        @pl.when(even)
        def _():
            hand(slope_n.at[0, m], slope_n.at[1, m], 9 + m)

    def transposes():
        for m in range(batches):
            at = pl.ds(m * local, local)
            nodes_t[:, m * count : (m + 1) * count] = nodes[m].T
            edges_t[:, at] = edges[m].T
            act_t[:, at] = act[m].T
            sum_t[:, m * count : (m + 1) * count] = sum_all[m].reshape(count, width).T
            agg = dot(sum_all[m].reshape(count, width), w_msg[0]).astype(BF)
            agg_t[:, m * count : (m + 1) * count] = agg.T
            node_act_t[:, m * count : (m + 1) * count] = node_act[m].T

    def edge_grad(li, m):
        return ge[m] if li == 0 else edge_out[0, m]

    def edge_base(li, m):
        base[m] = dot_t(edge_grad(li, m), w_msg[li])

    def chain(li, m):
        slot = li * batches + m
        span = pl.ds(m * local, local)
        at = pl.ds(m * count, count)
        grad_nodes = gh[li, m].reshape(count, width)
        delta = (dot_t(grad_nodes, w_out[li]) * slope_n[li, m]).astype(BF)
        node_delta[li, at, :] = delta
        mixed = dot(delta, w_am[li]).astype(BF)
        moved = ((base[m] + dot(recv_1[m], mixed)) * slope_e[li, m]).astype(BF)
        edge_delta[li, span, :] = moved
        if li == 1:

            @pl.when(section == 1)
            def _():
                hand(edge_delta.at[1, span], edge_delta.at[0, span], 2 + m)

        to_send = dot(send_t[m], moved).astype(BF)
        to_recv = dot(recv_t[m], moved).astype(BF)
        at_send[li, at, :] = to_send
        at_recv[li, at, :] = to_recv
        part = dot_t(to_send, w_send[li]) + dot_t(to_recv, w_recv[li])
        back_src[slot] = part.astype(BF).reshape(groups, rows, width)
        scatter(back_src.at[slot], back_buf.at[slot], s_back.at[slot], r_back.at[slot])
        back_buf[slot, me] = back_src[slot, me]
        if li == 1:

            @pl.when(section == 1)
            def _():
                hand_rest(m)

        edge_out[li, m] = (
            edge_grad(li, m).astype(F32) + dot_t(edge_delta[li, span, :], w_edge[li])
        ).astype(BF)
        if li == 0:
            hand(edge_out.at[0, m], ge.at[m], m)
        elif m == 0:

            @pl.when(section > 1)
            def _():
                edges_down(m)

    def hand_rest(m):
        at = pl.ds(m * count, count)
        hand(at_send.at[1, at], at_send.at[0, at], 4 + m)
        hand(at_recv.at[1, at], at_recv.at[0, at], 6 + m)
        hand(node_delta.at[1, at], node_delta.at[0, at], 8 + m)
        hand(gh.at[1, m], gh.at[0, m], 10 + m)

    def edges_down(m):
        remote(edge_out.at[1, m], ge.at[m], s_ge.at[m], r_ge.at[m], section - 2, me).start()

    def own_terms(li, m):
        own = node_delta[li, pl.ds(pl.multiple_of(m * count + me * rows, rows), rows), :]
        own_term[m] = gh[li, m, me].astype(F32) + dot_t(own, w_node[li])

    def finish(li, m):
        slot = li * batches + m
        take_bytes(back_buf.at[slot, pl.ds(0, groups - 1)], r_back.at[slot])
        summed = (own_term[m] + jnp.sum(back_buf[slot].astype(F32), axis=0)).astype(BF)
        node_out[li, m] = summed
        if li == 0:
            spread(node_out.at[0, m], gh.at[1, m, me], s_gh.at[2 + m], r_gh.at[2 + m])
            gh[1, m, me] = summed
        else:

            @pl.when(section > 1)
            def _():
                remote(
                    node_out.at[1, m], row_in.at[m], s_row.at[m], r_row.at[m], section - 2, me
                ).start()

            hand(node_out.at[1, m], node_out.at[0, m], 12 + m)

    def relay(m):
        take_bytes(row_in.at[m], r_row.at[m])
        spread(row_in.at[m], gh.at[0, m, me], s_gh.at[m], r_gh.at[m])
        gh[0, m, me] = row_in[m]

    def take_nodes(li, m):
        take_bytes(gh.at[li, m, pl.ds(0, groups - 1)], r_gh.at[li * batches + m])

    def make_grad(i):
        if i == 3:
            value = dot(act_t[...], ge[...].reshape(batches * local, width))
        elif i == 2:
            value = dot(edges_t[...], edge_delta[0])
        else:
            value = dot(nodes_t[...], (at_send if i == 0 else at_recv)[0])
        value = value.astype(BF)
        wide = width // 2
        left = value[:, :wide].reshape(side, side, share, wide)
        for k in range(side):
            grad_src[2 * i, k] = left[:, k]
        grad_src[2 * i + 1] = value[:, wide:].reshape(side, side, share, wide)

    steps = sorted(range(1, side), key=lambda step: -min(step, side - step))

    def along(half, step):
        return lax.rem((row_at if half else col_at) + step, side)

    def peer_along(half, spot):
        return spot * side + col_at if half else row_at * side + spot

    def send_grad(i):
        for half in range(2):
            slot = 2 * i + half
            for step in steps:
                spot = along(half, step)
                remote(
                    grad_src.at[slot, spot],
                    grad_mid.at[slot, along(half, 0)],
                    s_grad.at[slot],
                    r_grad.at[slot],
                    section,
                    peer_along(half, spot),
                ).start()

    def pass_grad(i):
        for half in range(2):
            slot = 2 * i + half
            here = along(half, 0)
            grad_mid[slot, here] = grad_src[slot, here]
            take_bytes(grad_mid.at[slot, pl.ds(0, side - 1)], r_grad.at[slot])
            half_src[slot] = jnp.sum(grad_mid[slot].astype(F32), axis=0).astype(BF)
            for step in steps:
                spot = along(1 - half, step)
                remote(
                    half_src.at[slot, spot],
                    half_buf.at[slot, along(1 - half, 0)],
                    s_half.at[slot],
                    r_half.at[slot],
                    section,
                    peer_along(1 - half, spot),
                ).start()
            half_buf[slot, along(1 - half, 0)] = half_src[slot, along(1 - half, 0)]

    node_forward(0)

    @pl.when(section < sections - 1)
    def _():
        node_forward(1)
        transposes()

    @pl.when(odd)
    def _():
        @pl.when(later)
        def _():
            take_bytes(ge.at[0], r_ge.at[0])
            edge_base(0, 0)
            relay(0)
            relay(1)
            take_nodes(0, 0)

        chain(0, 0)

        @pl.when(first)
        def _():
            node_forward(1)

        @pl.when(later)
        def _():
            take_bytes(ge.at[1], r_ge.at[1])
            edge_base(0, 1)
            take_nodes(0, 1)

        chain(0, 1)
        own_terms(0, 0)
        own_terms(0, 1)

        @pl.when(later)
        def _():
            for i in (2, 3):
                make_grad(i)

                @pl.when(section == 1)
                def _():
                    send_grad(i)

        finish(0, 0)
        finish(0, 1)

        @pl.when(later)
        def _():
            make_grad(0)

            @pl.when(section == 1)
            def _():
                send_grad(0)

        for i, w in enumerate(down):
            take_bytes(w.at[1], r_mate.at[i])
        edge_base(1, 0)
        edge_base(1, 1)

        @pl.when(first)
        def _():
            transposes()
            for i in (3, 2, 0):
                make_grad(i)

        make_grad(1)

        @pl.when(section == 1)
        def _():
            send_grad(1)
            pass_grad(2)
            pass_grad(3)

        for m in range(batches):
            take_bytes(slope_e.at[1, m], r_mate.at[7 + m])
            take_bytes(slope_n.at[1, m], r_mate.at[9 + m])
        take_nodes(1, 0)
        chain(1, 0)
        take_nodes(1, 1)
        chain(1, 1)
        own_terms(1, 0)
        own_terms(1, 1)
        finish(1, 0)

        @pl.when(section > 1)
        def _():
            edges_down(1)

        finish(1, 1)

        @pl.when(section > 1)
        def _():
            for m in range(batches):
                span = pl.ds(m * local, local)
                hand(edge_delta.at[1, span], edge_delta.at[0, span], 2 + m)
                hand_rest(m)

        for m in range(batches):
            hand(edge_out.at[1, m], edge_out.at[0, m], 14 + m)

        @pl.when(section > 1)
        def _():
            for i in (3, 2, 0, 1):
                send_grad(i)

    def take_outs():
        for m in range(batches):
            take_bytes(node_out.at[0, m], r_mate.at[12 + m])
            take_bytes(edge_out.at[0, m], r_mate.at[14 + m])

    @pl.when(even)
    def _():
        for m in range(batches):
            take_bytes(ge.at[m], r_mate.at[m])
        make_grad(3)
        last = section == 0
        for i, ref, at in ((2, edge_delta, 2), (0, at_send, 4), (1, at_recv, 6)):
            for m in range(batches):
                take_bytes(ref.at[0, pl.ds(m * local, local)], r_mate.at[at + m])
                if i == 2 and m == 0:

                    @pl.when(last)
                    def _():
                        send_grad(3)

            make_grad(i)

            @pl.when(last)
            def _():
                send_grad(i)

        for m in range(batches):
            take_bytes(node_delta.at[0, pl.ds(m * count, count)], r_mate.at[8 + m])
            take_bytes(gh.at[0, m], r_mate.at[10 + m])

        @pl.when(section > 0)
        def _():
            take_outs()
            for i in (3, 2, 0, 1):
                send_grad(i)

    agg_grad = dot_t(node_delta[0], w_agg[...]).astype(BF)
    grads[4] = dot(nodes_t[piece, :], node_delta[0])
    grads[5] = dot(agg_t[piece, :], node_delta[0])
    grads[6] = dot(node_act_t[piece, :], gh[0].reshape(batches * count, width))
    known = dot(sum_t[piece, :], agg_grad)
    @pl.when(section != 1)
    def _():
        pass_grad(3)
        pass_grad(2)

    pass_grad(0)
    pass_grad(1)

    @pl.when(section == 0)
    def _():
        take_outs()

    store_node = pltpu.make_async_copy(node_out.at[0], h_node_out, s_store.at[0])
    store_edge = pltpu.make_async_copy(edge_out.at[0], h_edge_out, s_store.at[1])
    store_node.start()
    store_edge.start()
    for i in (3, 2, 0, 1):
        for half in range(2):
            slot = 2 * i + half
            lanes = slice(half * (width // 2), (half + 1) * (width // 2))
            take_bytes(half_buf.at[slot, pl.ds(0, side - 1)], r_half.at[slot])
            total = jnp.sum(half_buf[slot].astype(F32), axis=0)
            grads[i, :, lanes] = total + known[:, lanes] if i == 3 else total
    store_grads = pltpu.make_async_copy(grads, h_grads, s_store.at[2])
    store_grads.start()

    for m in range(batches):
        take_bytes(sum_src.at[m, pl.ds(0, groups - 1)], s_sum.at[m])
        take_bytes(sum_all.at[m, pl.ds(0, groups - 1)], s_all.at[m])

    @pl.when(even)
    def _():
        for i, w in enumerate(down):
            take_bytes(w.at[0], s_mate.at[i])
        for m in range(batches):
            take_bytes(slope_e.at[0, m], s_mate.at[7 + m])
            take_bytes(slope_n.at[0, m], s_mate.at[9 + m])

    @pl.when(odd)
    def _():
        for m in range(batches):
            for li in range(2):
                slot = li * batches + m
                take_bytes(back_src.at[slot, pl.ds(0, groups - 1)], s_back.at[slot])
            take_bytes(gh.at[1, m, pl.ds(0, groups - 1)], s_gh.at[2 + m])
            take_bytes(ge.at[m], s_mate.at[m])
            for ref, at in ((edge_delta, 2), (at_send, 4), (at_recv, 6), (node_delta, 8)):
                take_bytes(ref.at[1, pl.ds(m * local, local)], s_mate.at[at + m])
            take_bytes(gh.at[1, m], s_mate.at[10 + m])
            take_bytes(node_out.at[1, m], s_mate.at[12 + m])
            take_bytes(edge_out.at[1, m], s_mate.at[14 + m])

        @pl.when(section > 1)
        def _():
            for m in range(batches):
                take_bytes(row_in.at[m], s_row.at[m])
                take_bytes(ge.at[m], s_ge.at[m])

        @pl.when(later)
        def _():
            for m in range(batches):
                take_bytes(gh.at[0, m, pl.ds(0, groups - 1)], s_gh.at[m])

    for slot in range(8):
        take_bytes(grad_src.at[slot, pl.ds(0, side - 1)], s_grad.at[slot])
        take_bytes(half_src.at[slot, pl.ds(0, side - 1)], s_half.at[slot])
    store_node.wait()
    store_edge.wait()
    store_grads.wait()


def write_kernel(*refs):
    node_in, edge_in, grads, node_out, edge_out, *outs = refs[:-5]
    node_at, edge_at, grad_at, sem_in, sem_out = refs[-5:]
    moves = [(edge_in.at[m], edge_at.at[m], edge_out.at[m]) for m in range(edge_in.shape[0])]
    moves += [(node_in, node_at, node_out)]
    moves += [(grads.at[i], grad_at.at[i], out) for i, out in enumerate(outs)]
    ins = [pltpu.make_async_copy(a, b, sem_in.at[i]) for i, (a, b, _) in enumerate(moves)]
    outs = [pltpu.make_async_copy(b, c, sem_out.at[i]) for i, (_, b, c) in enumerate(moves)]
    for copy in ins:
        copy.start()
    for copy, after in zip(ins, outs):
        copy.wait()
        after.start()
    for copy in outs:
        copy.wait()


def body(sections, groups, *args):
    nodes, edges, top_n, top_e, blocks, senders, receivers, *weights = args
    weights = [w[0] for w in weights]
    nodes, edges = nodes[0], edges[0]
    batches, count, width = nodes.shape
    local = edges.shape[1]
    hidden = weights[0].shape[1]
    rows, share = count // groups, width // groups
    vmem = pl.BlockSpec(memory_space=pltpu.VMEM)
    smem = pl.BlockSpec(memory_space=pltpu.SMEM)
    anyw = pl.BlockSpec(memory_space=pl.ANY)
    full = (batches, groups, rows, width)
    sem = pltpu.SemaphoreType.DMA
    V = pltpu.VMEM
    node_shape = jax.ShapeDtypeStruct((batches, rows, width), BF)
    edge_shape = jax.ShapeDtypeStruct((batches, local, width), BF)
    grad_shape = jax.ShapeDtypeStruct((share, hidden), F32)
    pair = (2, batches)
    side = round(groups**0.5)
    scratch = (
        [V((batches, count, width), BF), V((batches, local, width), BF)]
        + [V((2,) + full, BF), V((batches, local, width), BF)]
        + [V(w.shape if i == 5 else (2,) + w.shape, BF) for i, w in enumerate(weights)]
        + [V((2, hidden, hidden), BF)]
        + [V(pair + (rows, width), BF), V(pair + (local, width), BF)]
        + [V((7, share, hidden), F32)]
        + [V((batches, count, local), BF), V((batches, count, local), BF)]
        + [V((batches, local, count), BF), V((batches, local, hidden), BF)]
        + [V(pair + (local, hidden), F32), V(pair + (count, hidden), F32)]
        + [V((batches, count, hidden), BF)]
        + [V((2, batches * count, hidden), BF), V((2, batches * local, hidden), BF)]
        + [V((2, batches * count, hidden), BF), V((2, batches * count, hidden), BF)]
        + [V((batches, local, hidden), F32), V((batches, rows, width), F32)]
        + [V((batches, rows, width), BF)]
        + [V((width, batches * count), BF), V((width, batches * local), BF)]
        + [V((hidden, batches * local), BF), V((hidden, batches * count), BF)]
        + [V((width, batches * count), BF), V((hidden, batches * count), BF)]
        + [V(full, BF), V(full, BF), V((batches, rows, width), BF), V(full, BF)]
        + [V((2 * batches,) + full[1:], BF), V((2 * batches,) + full[1:], BF)]
        + [V((8, side, side, share, hidden // 2), BF)] * 2
        + [V((8, side, share, hidden // 2), BF)] * 2
        + [sem((11,)), sem((3,))]
        + [sem((batches,))] * 4
        + [sem((2 * batches,))] * 4
        + [sem((batches,))] * 4
        + [sem((16,))] * 2
        + [sem((8,))] * 4
        + [pltpu.SemaphoreType.REGULAR]
    )
    node_res, edge_res, grads = pl.pallas_call(
        functools.partial(kernel, sections, groups, batches),
        out_shape=[node_shape, edge_shape, jax.ShapeDtypeStruct((7, share, hidden), F32)],
        in_specs=[anyw] * 4 + [smem] + [vmem] * 2 + [anyw] * 7,
        out_specs=[anyw] * 3,
        scratch_shapes=scratch,
        compiler_params=pltpu.CompilerParams(
            collective_id=0, has_side_effects=True, vmem_limit_bytes=58 * 1024 * 1024
        ),
        name="window",
    )(
        nodes,
        edges,
        top_n.reshape(full),
        top_e,
        blocks,
        senders,
        receivers,
        *weights,
    )
    results = pl.pallas_call(
        write_kernel,
        out_shape=[node_shape, edge_shape] + [grad_shape] * 7,
        in_specs=[anyw] * 3,
        out_specs=[anyw] * 9,
        scratch_shapes=[
            V(node_shape.shape, BF),
            V(edge_shape.shape, BF),
            V((7, share, hidden), F32),
            sem((batches + 8,)),
            sem((batches + 8,)),
        ],
        name="write",
    )(node_res, edge_res, grads)
    return tuple(r[None] for r in results)


def solution(mesh):
    in_specs = (
        P("section", None, None, None),
        P("section", None, "edge", None),
        P(),
        P(None, "edge", None),
        P(None, "edge", None),
        P(None, "edge"),
        P(None, "edge"),
    ) + (P("section", None, None),) * 7
    out_specs = (
        P("section", None, "edge", None),
        P("section", None, "edge", None),
    ) + (P("section", "edge", None),) * 7
    step = functools.partial(body, mesh.shape["section"], mesh.shape["edge"])
    return jax.shard_map(step, mesh=mesh, in_specs=in_specs, out_specs=out_specs, check_vma=False)
```

```python
import functools

import jax
import jax.numpy as jnp
from jax import lax
from jax.experimental import pallas as pl
from jax.experimental.pallas import tpu as pltpu
from jax.sharding import PartitionSpec as P

MESH = pl.DeviceIdType.MESH
BF = jnp.bfloat16
F32 = jnp.float32


def dot(left, right):
    return jnp.dot(left, right, preferred_element_type=F32)


def dot_t(left, right):
    return lax.dot_general(left, right, (((1,), (1,)), ((), ())), preferred_element_type=F32)


def take_bytes(ref, sem):
    pltpu.make_async_copy(ref, ref, sem).wait()


def torus_offsets(side):
    def far(offset):
        return -sum(min(step, side - step) for step in offset)

    return sorted(((a, b) for a in range(side) for b in range(side)), key=far)


def kernel(sections, groups, batches, *refs):
    (
        h_nodes,
        h_edges,
        h_top_n,
        h_top_e,
        blocks,
        senders,
        receivers,
        h_send,
        h_recv,
        h_edge,
        h_msg,
        h_node,
        h_agg,
        h_out,
        h_node_out,
        h_edge_out,
        h_grads,
        nodes,
        edges,
        gh,
        ge,
        w_send,
        w_recv,
        w_edge,
        w_msg,
        w_node,
        w_agg,
        w_out,
        w_am,
        node_out,
        edge_out,
        grads,
        send_t,
        recv_t,
        recv_1,
        act,
        slope_e,
        slope_n,
        node_act,
        node_delta,
        edge_delta,
        at_send,
        at_recv,
        base,
        own_term,
        row_in,
        nodes_t,
        edges_t,
        act_t,
        sum_t,
        agg_t,
        node_act_t,
        sum_src,
        sum_buf,
        sum_row,
        sum_all,
        back_src,
        back_buf,
        grad_src,
        grad_mid,
        half_src,
        half_buf,
        s_load,
        s_store,
        s_sum,
        r_sum,
        s_all,
        r_all,
        s_back,
        r_back,
        s_gh,
        r_gh,
        s_row,
        r_row,
        s_ge,
        r_ge,
        s_mate,
        r_mate,
        s_grad,
        r_grad,
        s_half,
        r_half,
        turn,
    ) = refs
    section = lax.axis_index("section")
    me = lax.axis_index("edge")
    count, width = nodes.shape[1:]
    local = edges.shape[1]
    rows = count // groups
    share = width // groups
    side = round(groups**0.5)
    odd = lax.rem(section, 2) == 1
    even = lax.rem(section, 2) == 0
    mate = section + 1 - 2 * lax.rem(section, 2)
    first = section == sections - 1
    later = jnp.logical_and(odd, section < sections - 1)
    hands_down = jnp.logical_and(odd, section > 1)
    offsets = torus_offsets(side)
    row_at, col_at = me // side, lax.rem(me, side)

    def peer_at(offset):
        return lax.rem(row_at + offset[0], side) * side + lax.rem(col_at + offset[1], side)

    def remote(src, dst, ssem, rsem, where, peer):
        return pltpu.make_async_remote_copy(
            src_ref=src,
            dst_ref=dst,
            send_sem=ssem,
            recv_sem=rsem,
            device_id=(where, peer),
            device_id_type=MESH,
        )

    barrier = pltpu.get_barrier_semaphore()
    for offset in offsets[:-1]:
        pl.semaphore_signal(
            barrier, inc=1, device_id=(section, peer_at(offset)), device_id_type=MESH
        )
    pl.semaphore_signal(barrier, inc=1, device_id=(mate, me), device_id_type=MESH)

    @pl.when(later)
    def _():
        pl.semaphore_signal(barrier, inc=1, device_id=(section + 2, me), device_id_type=MESH)

    loads = [
        pltpu.make_async_copy(src, dst, s_load.at[i])
        for i, (src, dst) in enumerate(
            (
                (h_nodes, nodes),
                (h_edges, edges),
                (h_send, w_send.at[0]),
                (h_recv, w_recv.at[0]),
                (h_edge, w_edge.at[0]),
                (h_msg, w_msg.at[0]),
                (h_node, w_node.at[0]),
                (h_agg, w_agg),
                (h_out, w_out.at[0]),
            )
        )
    ]
    for copy in loads[:5]:
        copy.start()
    tops = [
        pltpu.make_async_copy(h_top_n, gh.at[0], s_load.at[len(loads)]),
        pltpu.make_async_copy(h_top_e, ge, s_load.at[len(loads) + 1]),
    ]


    def scatter(src, dst, ssem, rsem):
        for offset in offsets[:-1]:
            peer = peer_at(offset)
            remote(src.at[peer], dst.at[me], ssem, rsem, section, peer).start()

    def spread(src, dst, ssem, rsem):
        for offset in offsets[:-1]:
            remote(src, dst, ssem, rsem, section, peer_at(offset)).start()

    def hand(src, dst, i):
        remote(src, dst, s_mate.at[i], r_mate.at[i], mate, me).start()

    lane = lax.broadcasted_iota(jnp.int32, (1, local), 1)
    tile_len = local // blocks.shape[1]
    row_id = lax.broadcasted_iota(jnp.int32, (count, local), 0)
    piece = pl.ds(pl.multiple_of(me * share, share), share)

    for m in range(batches):
        for part, index, hot in ((0, senders, send_t), (1, receivers, recv_t)):
            block = jnp.zeros((1, local), jnp.int32)
            for k in range(blocks.shape[1]):
                block = jnp.where(lane // tile_len == k, blocks[m, k, part], block)
            ids = index[m : m + 1, :] + block * 128
            picked = jnp.where(row_id == ids, 1.0, 0.0).astype(F32)
            hot[m] = picked.astype(BF)
            if part == 1:
                recv_1[m] = picked.T.astype(BF)
        if m == 0:
            for copy in loads[:5]:
                copy.wait()
            for copy in loads[5:]:
                copy.start()

            @pl.when(first)
            def _():
                for copy in tops:
                    copy.start()

        feats = nodes[m]
        send_feats = lax.dot_general(
            send_t[m], feats, (((0,), (0,)), ((), ())), preferred_element_type=F32
        ).astype(BF)
        recv_feats = dot(recv_1[m], feats).astype(BF)
        pre = (
            dot(send_feats, w_send[0]) + dot(recv_feats, w_recv[0]) + dot(edges[m], w_edge[0])
        )
        sigma = jax.nn.sigmoid(pre)
        done = (pre * sigma).astype(BF)
        act[m] = done
        slope_e[0, m] = sigma * (1.0 + pre * (1.0 - sigma))
        sum_src[m] = dot(recv_t[m], done).astype(BF).reshape(groups, rows, width)
        if m == 0:
            pl.semaphore_wait(barrier, groups + hands_down.astype(jnp.int32))
        sum_buf[m, me] = sum_src[m, me]

        @pl.when(odd)
        def _():
            scatter(sum_src.at[m], sum_buf.at[m], s_sum.at[m], r_sum.at[m])
            if m == batches - 1:
                pl.semaphore_signal(turn, inc=1, device_id=(mate, me), device_id_type=MESH)

    for copy in loads[5:]:
        copy.wait()
    w_am[0] = lax.dot_general(
        w_agg[...], w_msg[0], (((0,), (1,)), ((), ())), preferred_element_type=F32
    ).astype(BF)
    down = (w_msg, w_send, w_recv, w_edge, w_node, w_out, w_am)

    @pl.when(even)
    def _():
        for i, w in enumerate(down):
            hand(w.at[0], w.at[1], i)
        for m in range(batches):
            hand(slope_e.at[0, m], slope_e.at[1, m], 7 + m)
        pl.semaphore_wait(turn, 1)
        for m in range(batches):
            scatter(sum_src.at[m], sum_buf.at[m], s_sum.at[m], r_sum.at[m])

    for m in range(batches):
        slope_n[0, m] = dot(nodes[m], w_node[0])

    @pl.when(first)
    def _():
        for copy in tops:
            copy.wait()
        for m in range(batches):
            base[m] = dot_t(ge[m], w_msg[0])

    for m in range(batches):
        take_bytes(sum_buf.at[m, pl.ds(0, groups - 1)], r_sum.at[m])
        summed = jnp.sum(sum_buf[m].astype(F32), axis=0).astype(BF)
        sum_row[m] = summed
        spread(sum_row.at[m], sum_all.at[m, me], s_all.at[m], r_all.at[m])
        sum_all[m, me] = summed

    def node_forward(m):
        take_bytes(sum_all.at[m, pl.ds(0, groups - 1)], r_all.at[m])
        node_pre = slope_n[0, m] + dot_t(sum_all[m].reshape(count, width), w_am[0])
        sigma = jax.nn.sigmoid(node_pre)
        node_act[m] = (node_pre * sigma).astype(BF)
        slope_n[0, m] = sigma * (1.0 + node_pre * (1.0 - sigma))

        @pl.when(even)
        def _():
            hand(slope_n.at[0, m], slope_n.at[1, m], 9 + m)

    def transposes():
        for m in range(batches):
            at = pl.ds(m * local, local)
            nodes_t[:, m * count : (m + 1) * count] = nodes[m].T
            edges_t[:, at] = edges[m].T
            act_t[:, at] = act[m].T
            sum_t[:, m * count : (m + 1) * count] = sum_all[m].reshape(count, width).T
            agg = dot(sum_all[m].reshape(count, width), w_msg[0]).astype(BF)
            agg_t[:, m * count : (m + 1) * count] = agg.T
            node_act_t[:, m * count : (m + 1) * count] = node_act[m].T

    def edge_grad(li, m):
        return ge[m] if li == 0 else edge_out[0, m]

    def edge_base(li, m):
        base[m] = dot_t(edge_grad(li, m), w_msg[li])

    def chain(li, m):
        slot = li * batches + m
        span = pl.ds(m * local, local)
        at = pl.ds(m * count, count)
        grad_nodes = gh[li, m].reshape(count, width)
        delta = (dot_t(grad_nodes, w_out[li]) * slope_n[li, m]).astype(BF)
        node_delta[li, at, :] = delta
        mixed = dot(delta, w_am[li]).astype(BF)
        moved = ((base[m] + dot(recv_1[m], mixed)) * slope_e[li, m]).astype(BF)
        edge_delta[li, span, :] = moved
        if li == 1:

            @pl.when(section == 1)
            def _():
                hand(edge_delta.at[1, span], edge_delta.at[0, span], 2 + m)

        to_send = dot(send_t[m], moved).astype(BF)
        to_recv = dot(recv_t[m], moved).astype(BF)
        at_send[li, at, :] = to_send
        at_recv[li, at, :] = to_recv
        part = dot_t(to_send, w_send[li]) + dot_t(to_recv, w_recv[li])
        back_src[slot] = part.astype(BF).reshape(groups, rows, width)
        scatter(back_src.at[slot], back_buf.at[slot], s_back.at[slot], r_back.at[slot])
        back_buf[slot, me] = back_src[slot, me]
        if li == 1:

            @pl.when(section == 1)
            def _():
                hand_rest(m)

        edge_out[li, m] = (
            edge_grad(li, m).astype(F32) + dot_t(edge_delta[li, span, :], w_edge[li])
        ).astype(BF)
        if li == 0:
            hand(edge_out.at[0, m], ge.at[m], m)
        elif m == 0:

            @pl.when(section > 1)
            def _():
                edges_down(m)

    def hand_rest(m):
        at = pl.ds(m * count, count)
        hand(at_send.at[1, at], at_send.at[0, at], 4 + m)
        hand(at_recv.at[1, at], at_recv.at[0, at], 6 + m)
        hand(node_delta.at[1, at], node_delta.at[0, at], 8 + m)
        hand(gh.at[1, m], gh.at[0, m], 10 + m)

    def edges_down(m):
        remote(edge_out.at[1, m], ge.at[m], s_ge.at[m], r_ge.at[m], section - 2, me).start()

    def own_terms(li, m):
        own = node_delta[li, pl.ds(pl.multiple_of(m * count + me * rows, rows), rows), :]
        own_term[m] = gh[li, m, me].astype(F32) + dot_t(own, w_node[li])

    def finish(li, m):
        slot = li * batches + m
        take_bytes(back_buf.at[slot, pl.ds(0, groups - 1)], r_back.at[slot])
        summed = (own_term[m] + jnp.sum(back_buf[slot].astype(F32), axis=0)).astype(BF)
        node_out[li, m] = summed
        if li == 0:
            spread(node_out.at[0, m], gh.at[1, m, me], s_gh.at[2 + m], r_gh.at[2 + m])
            gh[1, m, me] = summed
        else:

            @pl.when(section > 1)
            def _():
                remote(
                    node_out.at[1, m], row_in.at[m], s_row.at[m], r_row.at[m], section - 2, me
                ).start()

            hand(node_out.at[1, m], node_out.at[0, m], 12 + m)

    def relay(m):
        take_bytes(row_in.at[m], r_row.at[m])
        spread(row_in.at[m], gh.at[0, m, me], s_gh.at[m], r_gh.at[m])
        gh[0, m, me] = row_in[m]

    def take_nodes(li, m):
        take_bytes(gh.at[li, m, pl.ds(0, groups - 1)], r_gh.at[li * batches + m])

    def make_grad(i):
        if i == 3:
            value = dot(act_t[...], ge[...].reshape(batches * local, width))
        elif i == 2:
            value = dot(edges_t[...], edge_delta[0])
        else:
            value = dot(nodes_t[...], (at_send if i == 0 else at_recv)[0])
        value = value.astype(BF)
        wide = width // 2
        left = value[:, :wide].reshape(side, side, share, wide)
        for k in range(side):
            grad_src[2 * i, k] = left[:, k]
        grad_src[2 * i + 1] = value[:, wide:].reshape(side, side, share, wide)

    steps = sorted(range(1, side), key=lambda step: -min(step, side - step))

    def along(half, step):
        return lax.rem((row_at if half else col_at) + step, side)

    def peer_along(half, spot):
        return spot * side + col_at if half else row_at * side + spot

    def send_grad(i):
        for half in range(2):
            slot = 2 * i + half
            for step in steps:
                spot = along(half, step)
                remote(
                    grad_src.at[slot, spot],
                    grad_mid.at[slot, along(half, 0)],
                    s_grad.at[slot],
                    r_grad.at[slot],
                    section,
                    peer_along(half, spot),
                ).start()

    def pass_grad(i):
        for half in range(2):
            slot = 2 * i + half
            here = along(half, 0)
            grad_mid[slot, here] = grad_src[slot, here]
            take_bytes(grad_mid.at[slot, pl.ds(0, side - 1)], r_grad.at[slot])
            half_src[slot] = jnp.sum(grad_mid[slot].astype(F32), axis=0).astype(BF)
            for step in steps:
                spot = along(1 - half, step)
                remote(
                    half_src.at[slot, spot],
                    half_buf.at[slot, along(1 - half, 0)],
                    s_half.at[slot],
                    r_half.at[slot],
                    section,
                    peer_along(1 - half, spot),
                ).start()
            half_buf[slot, along(1 - half, 0)] = half_src[slot, along(1 - half, 0)]

    node_forward(0)

    @pl.when(section < sections - 1)
    def _():
        node_forward(1)
        transposes()

    @pl.when(odd)
    def _():
        @pl.when(later)
        def _():
            take_bytes(ge.at[0], r_ge.at[0])
            edge_base(0, 0)
            relay(0)
            relay(1)
            take_nodes(0, 0)

        chain(0, 0)

        @pl.when(first)
        def _():
            node_forward(1)

        @pl.when(later)
        def _():
            take_bytes(ge.at[1], r_ge.at[1])
            edge_base(0, 1)
            take_nodes(0, 1)

        chain(0, 1)
        own_terms(0, 0)
        own_terms(0, 1)

        @pl.when(later)
        def _():
            for i in (2, 3):
                make_grad(i)

                @pl.when(section == 1)
                def _():
                    send_grad(i)

        finish(0, 0)
        finish(0, 1)

        @pl.when(later)
        def _():
            make_grad(0)

            @pl.when(section == 1)
            def _():
                send_grad(0)

        for i, w in enumerate(down):
            take_bytes(w.at[1], r_mate.at[i])
        edge_base(1, 0)
        edge_base(1, 1)

        @pl.when(later)
        def _():
            make_grad(1)

        @pl.when(section == 1)
        def _():
            send_grad(1)
            pass_grad(2)
            pass_grad(3)

        for m in range(batches):
            take_bytes(slope_e.at[1, m], r_mate.at[7 + m])
            take_bytes(slope_n.at[1, m], r_mate.at[9 + m])
        take_nodes(1, 0)
        chain(1, 0)
        take_nodes(1, 1)
        chain(1, 1)
        own_terms(1, 0)
        own_terms(1, 1)
        finish(1, 0)

        @pl.when(section > 1)
        def _():
            edges_down(1)

        finish(1, 1)

        @pl.when(section > 1)
        def _():
            for m in range(batches):
                span = pl.ds(m * local, local)
                hand(edge_delta.at[1, span], edge_delta.at[0, span], 2 + m)
                hand_rest(m)

        for m in range(batches):
            hand(edge_out.at[1, m], edge_out.at[0, m], 14 + m)

        @pl.when(first)
        def _():
            transposes()
            for i in (3, 2, 0, 1):
                make_grad(i)

        @pl.when(section > 1)
        def _():
            for i in (3, 2, 0, 1):
                send_grad(i)

    def take_outs():
        for m in range(batches):
            take_bytes(node_out.at[0, m], r_mate.at[12 + m])
            take_bytes(edge_out.at[0, m], r_mate.at[14 + m])

    @pl.when(even)
    def _():
        for m in range(batches):
            take_bytes(ge.at[m], r_mate.at[m])
        make_grad(3)
        last = section == 0
        for i, ref, at in ((2, edge_delta, 2), (0, at_send, 4), (1, at_recv, 6)):
            for m in range(batches):
                take_bytes(ref.at[0, pl.ds(m * local, local)], r_mate.at[at + m])
                if i == 2 and m == 0:

                    @pl.when(last)
                    def _():
                        send_grad(3)

            make_grad(i)

            @pl.when(last)
            def _():
                send_grad(i)

        for m in range(batches):
            take_bytes(node_delta.at[0, pl.ds(m * count, count)], r_mate.at[8 + m])
            take_bytes(gh.at[0, m], r_mate.at[10 + m])

        @pl.when(section > 0)
        def _():
            take_outs()
            for i in (3, 2, 0, 1):
                send_grad(i)

    agg_grad = dot_t(node_delta[0], w_agg[...]).astype(BF)
    grads[4] = dot(nodes_t[piece, :], node_delta[0])
    grads[5] = dot(agg_t[piece, :], node_delta[0])
    grads[6] = dot(node_act_t[piece, :], gh[0].reshape(batches * count, width))
    known = dot(sum_t[piece, :], agg_grad)
    @pl.when(section != 1)
    def _():
        pass_grad(3)
        pass_grad(2)

    pass_grad(0)
    pass_grad(1)

    @pl.when(section == 0)
    def _():
        take_outs()

    store_node = pltpu.make_async_copy(node_out.at[0], h_node_out, s_store.at[0])
    store_edge = pltpu.make_async_copy(edge_out.at[0], h_edge_out, s_store.at[1])
    store_node.start()
    store_edge.start()
    for i in (3, 2, 0, 1):
        for half in range(2):
            slot = 2 * i + half
            lanes = slice(half * (width // 2), (half + 1) * (width // 2))
            take_bytes(half_buf.at[slot, pl.ds(0, side - 1)], r_half.at[slot])
            total = jnp.sum(half_buf[slot].astype(F32), axis=0)
            grads[i, :, lanes] = total + known[:, lanes] if i == 3 else total
    store_grads = pltpu.make_async_copy(grads, h_grads, s_store.at[2])
    store_grads.start()

    for m in range(batches):
        take_bytes(sum_src.at[m, pl.ds(0, groups - 1)], s_sum.at[m])
        take_bytes(sum_all.at[m, pl.ds(0, groups - 1)], s_all.at[m])

    @pl.when(even)
    def _():
        for i, w in enumerate(down):
            take_bytes(w.at[0], s_mate.at[i])
        for m in range(batches):
            take_bytes(slope_e.at[0, m], s_mate.at[7 + m])
            take_bytes(slope_n.at[0, m], s_mate.at[9 + m])

    @pl.when(odd)
    def _():
        for m in range(batches):
            for li in range(2):
                slot = li * batches + m
                take_bytes(back_src.at[slot, pl.ds(0, groups - 1)], s_back.at[slot])
            take_bytes(gh.at[1, m, pl.ds(0, groups - 1)], s_gh.at[2 + m])
            take_bytes(ge.at[m], s_mate.at[m])
            for ref, at in ((edge_delta, 2), (at_send, 4), (at_recv, 6), (node_delta, 8)):
                take_bytes(ref.at[1, pl.ds(m * local, local)], s_mate.at[at + m])
            take_bytes(gh.at[1, m], s_mate.at[10 + m])
            take_bytes(node_out.at[1, m], s_mate.at[12 + m])
            take_bytes(edge_out.at[1, m], s_mate.at[14 + m])

        @pl.when(section > 1)
        def _():
            for m in range(batches):
                take_bytes(row_in.at[m], s_row.at[m])
                take_bytes(ge.at[m], s_ge.at[m])

        @pl.when(later)
        def _():
            for m in range(batches):
                take_bytes(gh.at[0, m, pl.ds(0, groups - 1)], s_gh.at[m])

    for slot in range(8):
        take_bytes(grad_src.at[slot, pl.ds(0, side - 1)], s_grad.at[slot])
        take_bytes(half_src.at[slot, pl.ds(0, side - 1)], s_half.at[slot])
    store_node.wait()
    store_edge.wait()
    store_grads.wait()


def write_kernel(*refs):
    node_in, edge_in, grads, node_out, edge_out, *outs = refs[:-5]
    node_at, edge_at, grad_at, sem_in, sem_out = refs[-5:]
    moves = [(edge_in.at[m], edge_at.at[m], edge_out.at[m]) for m in range(edge_in.shape[0])]
    moves += [(node_in, node_at, node_out)]
    moves += [(grads.at[i], grad_at.at[i], out) for i, out in enumerate(outs)]
    ins = [pltpu.make_async_copy(a, b, sem_in.at[i]) for i, (a, b, _) in enumerate(moves)]
    outs = [pltpu.make_async_copy(b, c, sem_out.at[i]) for i, (_, b, c) in enumerate(moves)]
    for copy in ins:
        copy.start()
    for copy, after in zip(ins, outs):
        copy.wait()
        after.start()
    for copy in outs:
        copy.wait()


def body(sections, groups, *args):
    nodes, edges, top_n, top_e, blocks, senders, receivers, *weights = args
    weights = [w[0] for w in weights]
    nodes, edges = nodes[0], edges[0]
    batches, count, width = nodes.shape
    local = edges.shape[1]
    hidden = weights[0].shape[1]
    rows, share = count // groups, width // groups
    vmem = pl.BlockSpec(memory_space=pltpu.VMEM)
    smem = pl.BlockSpec(memory_space=pltpu.SMEM)
    anyw = pl.BlockSpec(memory_space=pl.ANY)
    full = (batches, groups, rows, width)
    sem = pltpu.SemaphoreType.DMA
    V = pltpu.VMEM
    node_shape = jax.ShapeDtypeStruct((batches, rows, width), BF)
    edge_shape = jax.ShapeDtypeStruct((batches, local, width), BF)
    grad_shape = jax.ShapeDtypeStruct((share, hidden), F32)
    pair = (2, batches)
    side = round(groups**0.5)
    scratch = (
        [V((batches, count, width), BF), V((batches, local, width), BF)]
        + [V((2,) + full, BF), V((batches, local, width), BF)]
        + [V(w.shape if i == 5 else (2,) + w.shape, BF) for i, w in enumerate(weights)]
        + [V((2, hidden, hidden), BF)]
        + [V(pair + (rows, width), BF), V(pair + (local, width), BF)]
        + [V((7, share, hidden), F32)]
        + [V((batches, count, local), BF), V((batches, count, local), BF)]
        + [V((batches, local, count), BF), V((batches, local, hidden), BF)]
        + [V(pair + (local, hidden), F32), V(pair + (count, hidden), F32)]
        + [V((batches, count, hidden), BF)]
        + [V((2, batches * count, hidden), BF), V((2, batches * local, hidden), BF)]
        + [V((2, batches * count, hidden), BF), V((2, batches * count, hidden), BF)]
        + [V((batches, local, hidden), F32), V((batches, rows, width), F32)]
        + [V((batches, rows, width), BF)]
        + [V((width, batches * count), BF), V((width, batches * local), BF)]
        + [V((hidden, batches * local), BF), V((hidden, batches * count), BF)]
        + [V((width, batches * count), BF), V((hidden, batches * count), BF)]
        + [V(full, BF), V(full, BF), V((batches, rows, width), BF), V(full, BF)]
        + [V((2 * batches,) + full[1:], BF), V((2 * batches,) + full[1:], BF)]
        + [V((8, side, side, share, hidden // 2), BF)] * 2
        + [V((8, side, share, hidden // 2), BF)] * 2
        + [sem((11,)), sem((3,))]
        + [sem((batches,))] * 4
        + [sem((2 * batches,))] * 4
        + [sem((batches,))] * 4
        + [sem((16,))] * 2
        + [sem((8,))] * 4
        + [pltpu.SemaphoreType.REGULAR]
    )
    node_res, edge_res, grads = pl.pallas_call(
        functools.partial(kernel, sections, groups, batches),
        out_shape=[node_shape, edge_shape, jax.ShapeDtypeStruct((7, share, hidden), F32)],
        in_specs=[anyw] * 4 + [smem] + [vmem] * 2 + [anyw] * 7,
        out_specs=[anyw] * 3,
        scratch_shapes=scratch,
        compiler_params=pltpu.CompilerParams(
            collective_id=0, has_side_effects=True, vmem_limit_bytes=58 * 1024 * 1024
        ),
        name="window",
    )(
        nodes,
        edges,
        top_n.reshape(full),
        top_e,
        blocks,
        senders,
        receivers,
        *weights,
    )
    results = pl.pallas_call(
        write_kernel,
        out_shape=[node_shape, edge_shape] + [grad_shape] * 7,
        in_specs=[anyw] * 3,
        out_specs=[anyw] * 9,
        scratch_shapes=[
            V(node_shape.shape, BF),
            V(edge_shape.shape, BF),
            V((7, share, hidden), F32),
            sem((batches + 8,)),
            sem((batches + 8,)),
        ],
        name="write",
    )(node_res, edge_res, grads)
    return tuple(r[None] for r in results)


def solution(mesh):
    in_specs = (
        P("section", None, None, None),
        P("section", None, "edge", None),
        P(),
        P(None, "edge", None),
        P(None, "edge", None),
        P(None, "edge"),
        P(None, "edge"),
    ) + (P("section", None, None),) * 7
    out_specs = (
        P("section", None, "edge", None),
        P("section", None, "edge", None),
    ) + (P("section", "edge", None),) * 7
    step = functools.partial(body, mesh.shape["section"], mesh.shape["edge"])
    return jax.shard_map(step, mesh=mesh, in_specs=in_specs, out_specs=out_specs, check_vma=False)
```
